512 devices in a mesh: ctx: 64 (over z, y_lo, core), fsdp: 8 (over y_hi, x).
Axes of the slice: x: 4, y: 8 (y_hi: 2, y_lo: 4; y = y_hi * 4 + y_lo), z: 8, core: 2. Of those that a mesh axis runs over, the one named last changes fastest.
Arguments:
- tokens: bfloat16 [8192, 4096], P('ctx', 'fsdp'), may hold values from -130 to 130, as said below
- w_query: bfloat16 [4096, 4096], P('ctx', 'fsdp'), may hold values from -0.09375 to 0.09375
- key_matrix: bfloat16 [4096, 1024], P('ctx', 'fsdp'), may hold values from -0.09375 to 0.09375
- value_matrix: bfloat16 [4096, 1024], P('ctx', 'fsdp'), may hold values from -0.09375 to 0.09375
- w_out: bfloat16 [4096, 4096], P('fsdp', 'ctx'), may hold values from -0.75 to 0.75
Outputs:
- mixed: bfloat16 [8192, 4096], P('ctx', 'fsdp')
The draws below stay inside these ranges and needn't reach their ends.
Inputs may be any that keep to these rules, and one draw needn't show every extreme that they name: `tokens`: no structure of the entries is promised.
All inputs are finite; a program needn't handle non-finite values.
Results may differ from the reference program's by a relative error of at most 0.014.
The reference program's roundings to bfloat16 on the way count: a program that leaves them out, or rounds other values in their place, can miss the bound.
Values may be sent and summed in bfloat16 or wider, within the bound.
A program may use at most 64 MiB of HBM per device.

```python
import math
import jax
import jax.numpy as jnp
from jax import lax

MODEL_WIDTH = 4096
QUERY_HEADS = 32
SHARED_HEADS = 8
HEAD_SIZE = 128
EVENT_WINDOW = 8192
N_FSDP = 8


def draw_tokens(key, part):
    noise_key = jax.random.fold_in(key, 11)
    gauss_rows = jax.random.truncated_normal(noise_key, -6.0, 6.0, (EVENT_WINDOW, MODEL_WIDTH), jnp.float32) * 1.5
    return gauss_rows.astype(jnp.bfloat16)


def levels(stream_key, extent, shards, smallest, largest):
    def one(axis_at, parts):
        draws = jax.random.uniform(jax.random.fold_in(jax.random.fold_in(stream_key, 6), axis_at), (parts,), jnp.float32, smallest / len(shards), largest / len(shards))
        return jnp.repeat(jnp.exp(draws), extent[axis_at] // parts).reshape((-1,) + (1,) * (len(extent) - axis_at - 1))

    factor_of = one(*shards[0])
    for cut in shards[1:]:
        factor_of = factor_of * one(*cut)
    return factor_of


def noise(key, extent, scale, reach, shards=(), kind=jnp.bfloat16):
    array = jax.random.normal(key, extent, jnp.float32) * scale
    if len(shards) > 0:
        array = levels(key, extent, shards, -0.22, 0.18) * array
    return jnp.clip(array, min=-reach, max=reach).astype(kind)


def setup_inputs(seed: int = 0) -> dict:
    streams_of = jax.random.split(jax.random.key(seed), 6)
    return {
        "tokens": draw_tokens(jax.random.fold_in(streams_of[5], 71), 0),
        "w_query": noise(streams_of[1], (MODEL_WIDTH, QUERY_HEADS * HEAD_SIZE), MODEL_WIDTH ** -0.5, 0.09375, ((0, 64), (1, 8))),
        "key_matrix": noise(streams_of[2], (MODEL_WIDTH, SHARED_HEADS * HEAD_SIZE), MODEL_WIDTH ** -0.5, 0.09375, ((0, 64), (1, 8))),
        "value_matrix": noise(streams_of[3], (MODEL_WIDTH, SHARED_HEADS * HEAD_SIZE), MODEL_WIDTH ** -0.5, 0.09375, ((0, 64), (1, 8))),
        "w_out": noise(streams_of[4], (QUERY_HEADS * HEAD_SIZE, MODEL_WIDTH), 64 ** -0.5, 0.75, ((0, 8), (1, 64))),
    }


def rotate_heads(values, positions):
    tok_count = values.shape[0]
    head_count = values.shape[1] // HEAD_SIZE
    half_dim = HEAD_SIZE // 2
    inverse_freq = jnp.power(jnp.float32(500000.0), -jnp.arange(half_dim, dtype=jnp.float32) * 2.0 / HEAD_SIZE)
    angles = positions.astype(jnp.float32)[:, None] * inverse_freq[None, :]
    cosine = jnp.cos(angles)[:, None, :]
    sine_table = jnp.sin(angles)[:, None, :]
    shaped = values.reshape(tok_count, head_count, HEAD_SIZE)
    first_half = shaped[:, :, :half_dim]
    second = shaped[:, :, half_dim:]
    turned = jnp.concatenate([first_half * cosine - second * sine_table, second * cosine + first_half * sine_table], axis=2)
    return turned.reshape(tok_count, head_count * HEAD_SIZE).astype(jnp.bfloat16)

def reference(tokens, w_query, key_matrix, value_matrix, w_out):
    positions = jnp.arange(EVENT_WINDOW, dtype=jnp.int32)
    queries = rotate_heads(jnp.dot(tokens, w_query, preferred_element_type=jnp.float32), positions)
    projected_keys = rotate_heads(jnp.dot(tokens, key_matrix, preferred_element_type=jnp.float32), positions)
    projected_values = jnp.dot(tokens, value_matrix, preferred_element_type=jnp.float32).astype(jnp.bfloat16)
    queries_per_group = QUERY_HEADS // SHARED_HEADS
    expanded_keys = jnp.repeat(projected_keys.reshape(EVENT_WINDOW, SHARED_HEADS, HEAD_SIZE).astype(jnp.float32), queries_per_group, axis=1)
    expanded_values = jnp.repeat(projected_values.reshape(EVENT_WINDOW, SHARED_HEADS, HEAD_SIZE).astype(jnp.float32), queries_per_group, axis=1)
    block_rows = min(512, EVENT_WINDOW)
    score_scale = 1.0 / math.sqrt(HEAD_SIZE)

    def attend(block_index):
        begin = (block_index * block_rows).astype(jnp.int32)
        query_block = lax.dynamic_slice_in_dim(queries, begin, block_rows, 0).reshape(block_rows, QUERY_HEADS, HEAD_SIZE).astype(jnp.float32)
        scores = jnp.einsum('qhd,khd->hqk', query_block, expanded_keys) * score_scale
        query_pos = begin + jnp.arange(block_rows, dtype=jnp.int32)
        allowed = positions[None, None, :] <= query_pos[None, :, None]
        masked = jnp.where(allowed, scores, jnp.float32(-1e+30))
        row_max = lax.optimization_barrier(jnp.max(masked, axis=2, keepdims=True))
        exp_weights = jnp.where(allowed, jnp.exp(masked - row_max), jnp.float32(0.0))
        row_total = lax.optimization_barrier(jnp.sum(exp_weights, axis=2))
        rounded = exp_weights.astype(jnp.bfloat16).astype(jnp.float32)
        summed = jnp.einsum('hqk,khd->hqd', rounded, expanded_values)
        normed = summed / row_total[:, :, None]
        return normed.transpose(1, 0, 2).reshape(block_rows, QUERY_HEADS * HEAD_SIZE).astype(jnp.bfloat16)
    attn_out = lax.map(attend, jnp.arange(EVENT_WINDOW // block_rows, dtype=jnp.int32)).reshape(EVENT_WINDOW, QUERY_HEADS * HEAD_SIZE)
    group_width = QUERY_HEADS * HEAD_SIZE // N_FSDP
    total_out = jnp.zeros((EVENT_WINDOW, MODEL_WIDTH), jnp.float32)
    for group_index in range(N_FSDP):
        low = group_index * group_width
        group_term = jnp.dot(attn_out[:, low:low + group_width], w_out[low:low + group_width], preferred_element_type=jnp.float32)
        rounded_term = lax.optimization_barrier(group_term.astype(jnp.bfloat16))
        total_out = total_out + rounded_term.astype(jnp.float32)
    return total_out.astype(jnp.bfloat16)
```

```python
import functools
import math

import jax
import jax.numpy as jnp
import numpy as np
from jax import lax
from jax.experimental import pallas as pl
from jax.experimental.pallas import tpu as pltpu
from jax.sharding import PartitionSpec as P

MESH = pl.DeviceIdType.MESH
HEAD = 128
HEADS = 4
NZ, NY = 8, 4
TOK = 128
SCALE2 = math.log2(math.e) / math.sqrt(HEAD)
REACH = ((4, 4, 3, 3), (3, 3, 4, 4))
W, KV, WO = 0, 1, 2


def kernel(
    tok, wq, wk, wv, wo, invf, out,
    xbuf, wbuf, kvbuf, wobuf, wo_in, qbuf, proj, mbuf, lbuf, acc, abuf, pbuf, rbuf, sbuf, ybuf,
    local, zsend, ysend, bsend, zrecv, brecv, tsend, trecv, rsend, rrecv, hsend, hrecv,
):
    c = lax.axis_index("ctx")
    f = lax.axis_index("fsdp")
    k = c % 2
    y = (c // 2) % NY
    z = c // (2 * NY)
    x = f % 4
    yh = f // 4

    def at(zz, yy, kk):
        return ((zz * NY + yy) * 2 + kk, f)

    def up(d, n):
        return (z + (n if d == 0 else NZ - n)) % NZ

    def yo(dy):
        return (y + dy) % NY

    bufs = (wbuf, kvbuf, wobuf)

    def zcopy(g, d, step, dy):
        zz, yy = up(1 - d, step), yo(dy)
        ref = bufs[g].at[zz, yy, k]
        return pltpu.make_async_remote_copy(
            src_ref=ref, dst_ref=ref, send_sem=zsend.at[g, d, step, dy], recv_sem=zrecv.at[g, zz, yy],
            device_id=at(up(d, 1), y, k), device_id_type=MESH,
        )

    def ycopy(g, dy):
        ref = bufs[g].at[z, y, k]
        return pltpu.make_async_remote_copy(
            src_ref=ref, dst_ref=ref, send_sem=ysend.at[g, dy - 1], recv_sem=zrecv.at[g, z, y],
            device_id=at(z, yo(dy), k), device_id_type=MESH,
        )

    def bcopy(g, zz):
        ref = bufs[g].at[zz, :, k]
        return pltpu.make_async_remote_copy(
            src_ref=ref, dst_ref=ref, send_sem=bsend.at[g, zz], recv_sem=brecv.at[g, zz],
            device_id=at(z, y, 1 - k), device_id_type=MESH,
        )

    def arrived(g, zz, yy):
        ref = bufs[g].at[zz, yy, k]
        pltpu.make_async_remote_copy(
            src_ref=ref, dst_ref=ref, send_sem=zsend.at[g, 0, 0, 0], recv_sem=zrecv.at[g, zz, yy],
            device_id=at(z, y, 1 - k), device_id_type=MESH,
        ).wait_recv()

    def paired(g, zz):
        ref = bufs[g].at[zz, :, 1 - k]
        pltpu.make_async_remote_copy(
            src_ref=ref, dst_ref=ref, send_sem=bsend.at[g, zz], recv_sem=brecv.at[g, zz],
            device_id=at(z, y, 1 - k), device_id_type=MESH,
        ).wait_recv()

    def open_y(g):
        for dy in (2, 1, 3):
            ycopy(g, dy).start()

    def open_z(g):
        for d in (0, 1):
            zcopy(g, d, 0, 0).start()

    def step0(g):
        for dy in (1, 2, 3):
            arrived(g, z, yo(dy))
            for d in (0, 1):
                zcopy(g, d, 0, dy).start()
        bcopy(g, z).start()

    def step(g, s):
        for dy in range(NY):
            for d in (0, 1):
                if s <= REACH[d][dy]:
                    arrived(g, up(1 - d, s), yo(dy))
                    if s < REACH[d][dy]:
                        zcopy(g, d, s, dy).start()
        bcopy(g, up(1, s)).start()
        if s < 4:
            bcopy(g, up(0, s)).start()

    def drain(g):
        for d in (0, 1):
            for dy in range(NY):
                for s in range(REACH[d][dy]):
                    zcopy(g, d, s, dy).wait_send()
        for dy in (1, 2, 3):
            ycopy(g, dy).wait_send()
        for s in range(NZ):
            bcopy(g, up(0, s)).wait_send()

    def tcopy(n, slot, peer):
        ref = xbuf.at[slot]
        return pltpu.make_async_remote_copy(
            src_ref=ref, dst_ref=ref, send_sem=tsend.at[n], recv_sem=trecv.at[slot],
            device_id=(c, peer), device_id_type=MESH,
        )

    def tok_arrived(slot):
        tcopy(0, slot, yh * 4 + (x + 1) % 4).wait_recv()

    other = 1 - yh
    xr = yh * 4 + (x + 1) % 4
    xl = yh * 4 + (x + 3) % 4
    twin = other * 4 + x
    twin_l = other * 4 + (x + 3) % 4
    twin_r = other * 4 + (x + 1) % 4
    tokens_out = (
        (0, f, twin), (1, f, xr), (2, f, xl),
        (3, xl, xr),
        (4, twin, xr), (5, twin, xl),
        (6, twin_r, xl),
    )

    mine = wbuf.at[z, y, k]
    copies = [
        pltpu.make_async_copy(tok, xbuf.at[f], local.at[0]),
        pltpu.make_async_copy(wq, mine.at[:, pl.ds(0, 512)], local.at[1]),
        pltpu.make_async_copy(wk, mine.at[:, pl.ds(512, 128)], local.at[2]),
        pltpu.make_async_copy(wv, mine.at[:, pl.ds(640, 128)], local.at[3]),
        pltpu.make_async_copy(wo, wo_in, local.at[4]),
    ]
    for copy in copies:
        copy.start()

    barrier = pltpu.get_barrier_semaphore()
    peers = [at(up(0, 1), y, k), at(up(1, 1), y, k), at(z, y, 1 - k)]
    peers += [at(z, yo(dy), k) for dy in (1, 2, 3)]
    peers += [(c, yh * 4 + (x + dx) % 4) for dx in (1, 2, 3)]
    peers += [(c, twin)]
    for peer in peers:
        pl.semaphore_signal(barrier, inc=1, device_id=peer, device_id_type=MESH)
    for copy in copies:
        copy.wait()
    pl.semaphore_wait(barrier, len(peers))

    open_z(W)
    open_y(W)
    for n in (0, 1, 2):
        tcopy(*tokens_out[n]).start()
    wobuf[z, y, k] = wo_in[...].astype(jnp.float32).T.astype(jnp.bfloat16)
    step0(W)
    open_y(WO)

    position = (c * TOK + lax.broadcasted_iota(jnp.int32, (TOK, HEAD), 0)).astype(jnp.float32)
    angle = position * invf[...]
    cosine = jnp.cos(angle)
    lane = lax.broadcasted_iota(jnp.int32, (TOK, HEAD), 1)
    sine = jnp.sin(angle) * jnp.where(lane < HEAD // 2, -1.0, 1.0).astype(jnp.float32)

    def multiply(zz, first=False):
        paired(W, zz)
        term = jnp.dot(
            xbuf[zz], wbuf[zz].reshape(512, 768), preferred_element_type=jnp.float32
        )
        proj[...] = term if first else proj[...] + term

    step(W, 1)
    tok_arrived(xl)
    tcopy(*tokens_out[3]).start()
    tok_arrived(xr)
    tok_arrived(twin)
    tcopy(*tokens_out[4]).start()
    tcopy(*tokens_out[5]).start()
    step(W, 2)
    tok_arrived(twin_r)
    tcopy(*tokens_out[6]).start()
    tok_arrived(twin_l)
    tok_arrived(yh * 4 + (x + 2) % 4)
    step(W, 3)
    open_z(WO)
    for dy in (1, 2, 3):
        arrived(WO, z, yo(dy))
        for d in (0, 1):
            zcopy(WO, d, 0, dy).start()
    bcopy(WO, z).start()
    tok_arrived(other * 4 + (x + 2) % 4)
    multiply(z, True)
    for s in (1, 2):
        multiply(up(1, s))
        multiply(up(0, s))
    step(W, 4)
    multiply(up(1, 3))
    multiply(up(0, 3))
    multiply(up(0, 4))

    def turned(column):
        piece = proj[:, pl.ds(column, HEAD)]
        return (piece * cosine + pltpu.roll(piece, HEAD // 2, 1) * sine).astype(jnp.bfloat16)

    kvbuf[z, y, k, 0] = turned(512)
    kvbuf[z, y, k, 1] = proj[:, pl.ds(640, HEAD)].astype(jnp.bfloat16)
    open_z(KV)
    open_y(KV)
    for h in range(HEADS):
        qbuf[pl.ds(h * TOK, TOK), :] = turned(h * HEAD)

    rows = 256
    keys = NY * 2 * TOK

    def attend(zz, first=False):
        paired(KV, zz)

        def some():
            def body(i, carry):
                at_rows = pl.ds(pl.multiple_of(i * rows, rows), rows)
                key = kvbuf[zz, :, :, 0].reshape(keys, HEAD)
                value = kvbuf[zz, :, :, 1].reshape(keys, HEAD)
                score = lax.dot_general(
                    qbuf[at_rows, :], key, (((1,), (1,)), ((), ())), preferred_element_type=jnp.float32
                )
                if first:
                    key_at = lax.broadcasted_iota(jnp.int32, (rows, keys), 1)
                    query_at = (y * 2 + k) * TOK + lax.broadcasted_iota(jnp.int32, (rows, keys), 0) % TOK
                    score = jnp.where(key_at <= query_at, score, jnp.float32(-1e30))
                top = jnp.max(score, axis=1, keepdims=True)
                if first:
                    new = jnp.broadcast_to(top, (rows, HEAD))
                else:
                    old = mbuf[at_rows, :]
                    new = jnp.maximum(old, top)
                exps = jnp.exp2(score * SCALE2 - jnp.tile(new * SCALE2, (1, keys // HEAD)))
                total = jnp.sum(exps, axis=1, keepdims=True)
                summed = jnp.dot(exps.astype(jnp.bfloat16), value, preferred_element_type=jnp.float32)
                if first:
                    lbuf[at_rows, :] = jnp.broadcast_to(total, (rows, HEAD))
                    acc[at_rows, :] = summed
                else:
                    factor = jnp.exp2((old - new) * SCALE2)
                    lbuf[at_rows, :] = lbuf[at_rows, :] * factor + total
                    acc[at_rows, :] = acc[at_rows, :] * factor + summed
                mbuf[at_rows, :] = new
                return carry

            lax.fori_loop(0, HEADS * TOK // rows, body, 0)

        if first:
            some()
        else:
            pl.when(zz <= z)(some)

    step0(KV)
    step(KV, 1)
    attend(z, True)
    step(KV, 2)
    attend(up(1, 1))
    attend(up(0, 1))
    step(KV, 3)
    step(WO, 1)
    attend(up(1, 2))
    attend(up(0, 2))
    step(KV, 4)
    step(WO, 2)
    attend(up(1, 3))
    attend(up(0, 3))
    step(WO, 3)
    attend(up(0, 4))
    for h in range(HEADS):
        at_rows = pl.ds(h * TOK, TOK)
        abuf[:, pl.ds(h * HEAD, HEAD)] = (acc[at_rows, :] / lbuf[at_rows, :]).astype(jnp.bfloat16)
    step(WO, 4)
    for s in range(NZ):
        paired(WO, up(0, s))

    def block(slot):
        return lax.dot_general(
            abuf[...], wobuf[slot].reshape(512, 512), (((1,), (1,)), ((), ())),
            preferred_element_type=jnp.float32,
        ).astype(jnp.bfloat16)

    def rcopy(j, dx):
        there = (x + dx) % 4
        return pltpu.make_async_remote_copy(
            src_ref=pbuf.at[j, dx], dst_ref=rbuf.at[j, dx - 1], send_sem=rsend.at[j, dx - 1],
            recv_sem=rrecv.at[j, dx - 1], device_id=(c, yh * 4 + there), device_id_type=MESH,
        )

    for j, half in ((0, other), (1, yh)):
        for dx in (2, 1, 3, 0):
            pbuf[j, dx] = block(half * 4 + (x + dx) % 4)
            if dx:
                rcopy(j, dx).start()

    def summed_over_x(j):
        total = pbuf[j, 0].astype(jnp.float32)
        for dx in (1, 3, 2):
            rcopy(j, dx).wait_recv()
            total = total + rbuf[j, dx - 1].astype(jnp.float32)
        return total

    swap = pltpu.make_async_remote_copy(
        src_ref=sbuf, dst_ref=ybuf, send_sem=hsend.at[0], recv_sem=hrecv.at[0],
        device_id=(c, twin), device_id_type=MESH,
    )
    sbuf[...] = summed_over_x(0).astype(jnp.bfloat16)
    swap.start()
    proj[:, pl.ds(0, 512)] = summed_over_x(1)
    for g in (W, KV, WO):
        drain(g)
    for entry in tokens_out:
        tcopy(*entry).wait_send()
    for j in (0, 1):
        for dx in (1, 2, 3):
            rcopy(j, dx).wait_send()
    swap.wait()
    out[...] = (proj[:, pl.ds(0, 512)] + ybuf[...].astype(jnp.float32)).astype(jnp.bfloat16)


def body(tokens, w_query, key_matrix, value_matrix, w_out):
    half = HEAD // 2
    inverse_freq = np.power(
        np.float32(500000.0), -np.arange(half, dtype=np.float32) * np.float32(2.0) / np.float32(HEAD)
    ).astype(np.float32)
    table = jnp.asarray(np.concatenate([inverse_freq, inverse_freq])[None, :])
    hbm = pl.BlockSpec(memory_space=pl.ANY)
    vmem = pl.BlockSpec(memory_space=pltpu.VMEM)
    bf16, f32 = jnp.bfloat16, jnp.float32
    dma = pltpu.SemaphoreType.DMA
    return pl.pallas_call(
        kernel,
        out_shape=jax.ShapeDtypeStruct((TOK, 512), bf16),
        in_specs=[hbm] * 5 + [vmem],
        out_specs=vmem,
        scratch_shapes=[
            pltpu.VMEM((8, TOK, 512), bf16),
            pltpu.VMEM((NZ, NY, 2, 64, 768), bf16),
            pltpu.VMEM((NZ, NY, 2, 2, TOK, HEAD), bf16),
            pltpu.VMEM((NZ, NY, 2, 64, 512), bf16),
            pltpu.VMEM((512, 64), bf16),
            pltpu.VMEM((HEADS * TOK, HEAD), bf16),
            pltpu.VMEM((TOK, 768), f32),
            pltpu.VMEM((HEADS * TOK, HEAD), f32),
            pltpu.VMEM((HEADS * TOK, HEAD), f32),
            pltpu.VMEM((HEADS * TOK, HEAD), f32),
            pltpu.VMEM((TOK, 512), bf16),
            pltpu.VMEM((2, 4, TOK, 512), bf16),
            pltpu.VMEM((2, 3, TOK, 512), bf16),
            pltpu.VMEM((TOK, 512), bf16),
            pltpu.VMEM((TOK, 512), bf16),
            dma((5,)),
            dma((3, 2, 4, 4)),
            dma((3, 3)),
            dma((3, NZ)),
            dma((3, NZ, NY)),
            dma((3, NZ)),
            dma((7,)),
            dma((8,)),
            dma((2, 3)),
            dma((2, 3)),
            dma((1,)),
            dma((1,)),
        ],
        compiler_params=pltpu.CompilerParams(
            collective_id=0, has_side_effects=True, vmem_limit_bytes=50 * 2**20
        ),
    )(tokens, w_query, key_matrix, value_matrix, w_out, table)


def solution(mesh):
    in_specs = (
        P("ctx", "fsdp"),
        P("ctx", "fsdp"),
        P("ctx", "fsdp"),
        P("ctx", "fsdp"),
        P("fsdp", "ctx"),
    )
    out_specs = P("ctx", "fsdp")
    return jax.shard_map(body, mesh=mesh, in_specs=in_specs, out_specs=out_specs, check_vma=False)
```

```python
import functools
import math

import jax
import jax.numpy as jnp
import numpy as np
from jax import lax
from jax.experimental import pallas as pl
from jax.experimental.pallas import tpu as pltpu
from jax.sharding import PartitionSpec as P

MESH = pl.DeviceIdType.MESH
HEAD = 128
HEADS = 4
NZ, NY = 8, 4
TOK = 128
SCALE2 = math.log2(math.e) / math.sqrt(HEAD)
REACH = ((4, 4, 3, 3), (3, 3, 4, 4))
WKV, WQ, KV, WO = 0, 1, 2, 3
COLUMNS = (4, 4, 4, 1)


def kernel(
    tok, wq, wk, wv, wo, invf, out,
    xbuf, wkvbuf, wqbuf, kvbuf, wobuf, table, qbuf, proj, mbuf, lbuf, acc, abuf, pbuf, rbuf, sbuf, ybuf,
    local, zsend, ysend, bsend, zrecv, brecv, tsend, trecv, asend, arecv, rsend, rrecv, hsend, hrecv,
):
    c = lax.axis_index("ctx")
    f = lax.axis_index("fsdp")
    k = c % 2
    y = (c // 2) % NY
    z = c // (2 * NY)
    x = f % 4
    yh = f // 4

    def at(zz, yy, kk):
        return ((zz * NY + yy) * 2 + kk, f)

    def up(d, n):
        return (z + (n if d == 0 else NZ - n)) % NZ

    near = (y, y + 1 - 2 * (y % 2), 2 - y // 2, 3 - 3 * (y // 2))
    bufs = (wkvbuf, wqbuf, kvbuf)

    def shard(g, zz, yy):
        return wobuf.at[zz, k] if g == WO else bufs[g].at[zz, yy, k]

    def zcopy(g, d, step, n):
        zz, yy = up(1 - d, step), near[n]
        ref = shard(g, zz, yy)
        return pltpu.make_async_remote_copy(
            src_ref=ref, dst_ref=ref, send_sem=zsend.at[g, d, step, n], recv_sem=zrecv.at[g, zz, yy],
            device_id=at(up(d, 1), y, k), device_id_type=MESH,
        )

    def ycopy(g, n):
        ref = shard(g, z, y)
        return pltpu.make_async_remote_copy(
            src_ref=ref, dst_ref=ref, send_sem=ysend.at[g, n - 1], recv_sem=zrecv.at[g, z, y],
            device_id=at(z, near[n], k), device_id_type=MESH,
        )

    def bcopy(g, zz, kk):
        ref = wobuf.at[:, kk] if g == WO else bufs[g].at[zz, :, kk]
        return pltpu.make_async_remote_copy(
            src_ref=ref, dst_ref=ref, send_sem=bsend.at[g, zz], recv_sem=brecv.at[g, zz],
            device_id=at(z, y, 1 - k), device_id_type=MESH,
        )

    def arrived(g, zz, yy):
        ref = shard(g, zz, yy)
        pltpu.make_async_remote_copy(
            src_ref=ref, dst_ref=ref, send_sem=zsend.at[g, 0, 0, 0], recv_sem=zrecv.at[g, zz, yy],
            device_id=at(z, y, 1 - k), device_id_type=MESH,
        ).wait_recv()

    def paired(g, zz):
        bcopy(g, zz, 1 - k).wait_recv()

    def open_y(g):
        for n in (1, 2, 3):
            ycopy(g, n).start()

    def open_z(g):
        for d in (0, 1):
            zcopy(g, d, 0, 0).start()

    def step0(g):
        for n in (1, 2, 3):
            arrived(g, z, near[n])
            for d in (0, 1):
                zcopy(g, d, 0, n).start()
        bcopy(g, z, k).start()

    def step(g, s):
        for n in range(COLUMNS[g]):
            for d in (0, 1):
                if s <= REACH[d][n]:
                    arrived(g, up(1 - d, s), near[n])
                    if s < REACH[d][n]:
                        zcopy(g, d, s, n).start()
        if g != WO:
            bcopy(g, up(1, s), k).start()
            if s < 4:
                bcopy(g, up(0, s), k).start()
        elif s == 4:
            bcopy(g, 0, k).start()

    def drain(g):
        for d in (0, 1):
            for n in range(COLUMNS[g]):
                for s in range(REACH[d][n]):
                    zcopy(g, d, s, n).wait_send()
        if g == WO:
            bcopy(g, 0, k).wait_send()
            return
        for n in (1, 2, 3):
            ycopy(g, n).wait_send()
        for s in range(NZ):
            bcopy(g, up(0, s), k).wait_send()

    def tcopy(n, slot, peer):
        ref = xbuf.at[slot]
        return pltpu.make_async_remote_copy(
            src_ref=ref, dst_ref=ref, send_sem=tsend.at[n], recv_sem=trecv.at[slot],
            device_id=(c, peer), device_id_type=MESH,
        )

    def tok_arrived(slot):
        tcopy(0, slot, yh * 4 + (x + 1) % 4).wait_recv()

    other = 1 - yh
    xr = yh * 4 + (x + 1) % 4
    xl = yh * 4 + (x + 3) % 4
    twin = other * 4 + x
    twin_l = other * 4 + (x + 3) % 4
    twin_r = other * 4 + (x + 1) % 4
    tokens_out = (
        (0, f, twin), (1, f, xr), (2, f, xl),
        (3, xl, xr),
        (4, twin, xr), (5, twin, xl),
        (6, twin_r, xl),
    )

    mine = wkvbuf.at[z, y, k]
    copies = [
        pltpu.make_async_copy(wk, mine.at[:, pl.ds(0, HEAD)], local.at[0]),
        pltpu.make_async_copy(wv, mine.at[:, pl.ds(HEAD, HEAD)], local.at[1]),
        pltpu.make_async_copy(wo, wobuf.at[z, k], local.at[2]),
        pltpu.make_async_copy(wq, wqbuf.at[z, y, k], local.at[3]),
        pltpu.make_async_copy(tok, xbuf.at[f], local.at[4]),
        pltpu.make_async_copy(invf, table, local.at[5]),
    ]
    for copy in copies:
        copy.start()

    barrier = pltpu.get_barrier_semaphore()
    peers = [at(up(0, 1), y, k), at(up(1, 1), y, k), at(z, y, 1 - k)]
    peers += [at(z, near[n], k) for n in (1, 2, 3)]
    peers += [(c, yh * 4 + (x + dx) % 4) for dx in (1, 2, 3)]
    peers += [((z * NY + near[n]) * 2 + k, twin) for n in (0, 1, 2, 3)]
    for peer in peers:
        pl.semaphore_signal(barrier, inc=1, device_id=peer, device_id_type=MESH)
    for copy in copies:
        copy.wait()
    pl.semaphore_wait(barrier, len(peers))

    open_z(WKV)
    open_y(WKV)
    open_z(WO)
    open_y(WQ)
    tcopy(*tokens_out[1]).start()
    tcopy(*tokens_out[2]).start()
    step0(WKV)
    open_z(WQ)
    step(WKV, 1)
    step(WO, 1)
    step0(WQ)
    tcopy(*tokens_out[0]).start()
    step(WKV, 2)
    step(WO, 2)
    tok_arrived(xl)
    tcopy(*tokens_out[3]).start()
    tok_arrived(xr)
    step(WKV, 3)
    step(WO, 3)
    step(WQ, 1)
    step(WKV, 4)
    step(WO, 4)

    position = (c * TOK + lax.broadcasted_iota(jnp.int32, (TOK, HEAD), 0)).astype(jnp.float32)
    angle = position * table[...]
    cosine = jnp.cos(angle)
    lane = lax.broadcasted_iota(jnp.int32, (TOK, HEAD), 1)
    sine = jnp.sin(angle) * jnp.where(lane < HEAD // 2, -1.0, 1.0).astype(jnp.float32)

    def turned(piece):
        return (piece * cosine + pltpu.roll(piece, HEAD // 2, 1) * sine).astype(jnp.bfloat16)

    tok_arrived(twin)
    tcopy(*tokens_out[4]).start()
    tcopy(*tokens_out[5]).start()
    step(WQ, 2)
    tok_arrived(twin_r)
    tcopy(*tokens_out[6]).start()
    tok_arrived(twin_l)
    tok_arrived(yh * 4 + (x + 2) % 4)
    tok_arrived(other * 4 + (x + 2) % 4)

    for s in range(NZ):
        paired(WKV, up(0, s))
    both = jnp.zeros((TOK, 2 * HEAD), jnp.float32)
    for s in range(NZ):
        both += jnp.dot(xbuf[s], wkvbuf[s].reshape(512, 2 * HEAD), preferred_element_type=jnp.float32)
    kvbuf[z, y, k, 0] = turned(both[:, :HEAD])
    kvbuf[z, y, k, 1] = both[:, HEAD:].astype(jnp.bfloat16)
    open_z(KV)
    open_y(KV)

    def multiply(zz, first=False):
        paired(WQ, zz)
        term = jnp.dot(xbuf[zz], wqbuf[zz].reshape(512, 512), preferred_element_type=jnp.float32)
        proj[...] = term if first else proj[...] + term

    step(WQ, 3)
    multiply(z, True)
    multiply(up(1, 1))
    multiply(up(0, 1))
    step0(KV)
    multiply(up(1, 2))
    multiply(up(0, 2))
    step(WQ, 4)
    step(KV, 1)
    multiply(up(1, 3))
    multiply(up(0, 3))
    multiply(up(0, 4))
    for h in range(HEADS):
        qbuf[pl.ds(h * TOK, TOK), :] = turned(proj[:, pl.ds(h * HEAD, HEAD)])

    rows = 256
    keys = NY * 2 * TOK

    def attend(zz, first=False):
        paired(KV, zz)

        def some():
            def body(i, carry):
                at_rows = pl.ds(pl.multiple_of(i * rows, rows), rows)
                key = kvbuf[zz, :, :, 0].reshape(keys, HEAD)
                value = kvbuf[zz, :, :, 1].reshape(keys, HEAD)
                score = lax.dot_general(
                    qbuf[at_rows, :], key, (((1,), (1,)), ((), ())), preferred_element_type=jnp.float32
                )
                if first:
                    key_at = lax.broadcasted_iota(jnp.int32, (rows, keys), 1)
                    query_at = (y * 2 + k) * TOK + lax.broadcasted_iota(jnp.int32, (rows, keys), 0) % TOK
                    score = jnp.where(key_at <= query_at, score, jnp.float32(-1e30))
                top = jnp.max(score, axis=1, keepdims=True)
                if first:
                    new = jnp.broadcast_to(top, (rows, HEAD))
                else:
                    old = mbuf[at_rows, :]
                    new = jnp.maximum(old, top)
                exps = jnp.exp2(score * SCALE2 - jnp.tile(new * SCALE2, (1, keys // HEAD)))
                total = jnp.sum(exps, axis=1, keepdims=True)
                summed = jnp.dot(exps.astype(jnp.bfloat16), value, preferred_element_type=jnp.float32)
                if first:
                    lbuf[at_rows, :] = jnp.broadcast_to(total, (rows, HEAD))
                    acc[at_rows, :] = summed
                else:
                    factor = jnp.exp2((old - new) * SCALE2)
                    lbuf[at_rows, :] = lbuf[at_rows, :] * factor + total
                    acc[at_rows, :] = acc[at_rows, :] * factor + summed
                mbuf[at_rows, :] = new
                return carry

            lax.fori_loop(0, HEADS * TOK // rows, body, 0)

        if first:
            some()
        else:
            pl.when(zz <= z)(some)

    attend(z, True)
    step(KV, 2)
    attend(up(1, 1))
    attend(up(0, 1))
    step(KV, 3)
    attend(up(1, 2))
    attend(up(0, 2))
    step(KV, 4)
    attend(up(1, 3))
    attend(up(0, 3))
    attend(up(0, 4))
    for h in range(HEADS):
        at_rows = pl.ds(h * TOK, TOK)
        abuf[y, :, pl.ds(h * HEAD, HEAD)] = (acc[at_rows, :] / lbuf[at_rows, :]).astype(jnp.bfloat16)

    def acopy(n, yy):
        ref = abuf.at[yy]
        return pltpu.make_async_remote_copy(
            src_ref=ref, dst_ref=ref, send_sem=asend.at[n - 1], recv_sem=arecv.at[yy],
            device_id=at(z, near[n], k), device_id_type=MESH,
        )

    for n in (1, 2, 3):
        acopy(n, y).start()
    bcopy(WO, 0, 1 - k).wait_recv()

    def rcopy(n, dx):
        there = (x + dx) % 4
        return pltpu.make_async_remote_copy(
            src_ref=pbuf.at[n, :, there], dst_ref=rbuf.at[n, dx - 1], send_sem=rsend.at[n, dx - 1],
            recv_sem=rrecv.at[n, dx - 1], device_id=(c, yh * 4 + there), device_id_type=MESH,
        )

    def make_terms(n):
        if n:
            acopy(n, near[n]).wait_recv()
        terms = lax.dot_general(
            abuf[near[n]], wobuf[...].reshape(1024, 512), (((1,), (1,)), ((), ())),
            preferred_element_type=jnp.float32,
        ).astype(jnp.bfloat16)
        for slot in range(8):
            pbuf[n, slot // 4, slot % 4] = terms[:, slot * HEAD:(slot + 1) * HEAD]
        for dx in (2, 1, 3):
            rcopy(n, dx).start()

    def hcopy(n, j):
        half = (other, yh)[j]
        return pltpu.make_async_remote_copy(
            src_ref=sbuf.at[n, j], dst_ref=ybuf.at[yh, y], send_sem=hsend.at[n, j], recv_sem=hrecv.at[yh, y],
            device_id=((z * NY + near[n]) * 2 + k, half * 4 + x), device_id_type=MESH,
        )

    def sum_over_x(n):
        for dx in (1, 3, 2):
            rcopy(n, dx).wait_recv()
        for j, half in ((0, other), (1, yh)):
            total = pbuf[n, half, x].astype(jnp.float32)
            for dx in (1, 2, 3):
                total = total + rbuf[n, dx - 1, half].astype(jnp.float32)
            if n == 0 and j == 1:
                ybuf[yh, y] = total.astype(jnp.bfloat16)
            else:
                sbuf[n, j] = total.astype(jnp.bfloat16)
                hcopy(n, j).start()

    make_terms(0)
    make_terms(1)
    sum_over_x(0)
    make_terms(2)
    sum_over_x(1)
    make_terms(3)
    sum_over_x(2)
    sum_over_x(3)
    for g in (WKV, WQ, KV, WO):
        drain(g)
    for entry in tokens_out:
        tcopy(*entry).wait_send()
    for n in (1, 2, 3):
        acopy(n, y).wait_send()
    for n in range(NY):
        for dx in (1, 2, 3):
            rcopy(n, dx).wait_send()
        for j in (0, 1):
            if n or j == 0:
                hcopy(n, j).wait_send()
                ref = ybuf.at[(other, yh)[j], near[n]]
                pltpu.make_async_remote_copy(
                    src_ref=ref, dst_ref=ref, send_sem=hsend.at[n, j],
                    recv_sem=hrecv.at[(other, yh)[j], near[n]],
                    device_id=(c, twin), device_id_type=MESH,
                ).wait_recv()
    for n in range(NY):
        out[:, pl.ds(n * HEAD, HEAD)] = (
            ybuf[0, n].astype(jnp.float32) + ybuf[1, n].astype(jnp.float32)
        ).astype(jnp.bfloat16)


def body(tokens, w_query, key_matrix, value_matrix, w_out):
    half = HEAD // 2
    inverse_freq = np.power(
        np.float32(500000.0), -np.arange(half, dtype=np.float32) * np.float32(2.0) / np.float32(HEAD)
    ).astype(np.float32)
    table = jnp.asarray(np.concatenate([inverse_freq, inverse_freq])[None, :])
    hbm = pl.BlockSpec(memory_space=pltpu.HBM)
    vmem = pl.BlockSpec(memory_space=pltpu.VMEM)
    bf16, f32 = jnp.bfloat16, jnp.float32
    dma = pltpu.SemaphoreType.DMA
    return pl.pallas_call(
        kernel,
        out_shape=jax.ShapeDtypeStruct((TOK, 512), bf16),
        in_specs=[hbm] * 6,
        out_specs=vmem,
        scratch_shapes=[
            pltpu.VMEM((8, TOK, 512), bf16),
            pltpu.VMEM((NZ, NY, 2, 64, 2 * HEAD), bf16),
            pltpu.VMEM((NZ, NY, 2, 64, 512), bf16),
            pltpu.VMEM((NZ, NY, 2, 2, TOK, HEAD), bf16),
            pltpu.VMEM((NZ, 2, 64, 512), bf16),
            pltpu.VMEM((1, HEAD), f32),
            pltpu.VMEM((HEADS * TOK, HEAD), bf16),
            pltpu.VMEM((TOK, 512), f32),
            pltpu.VMEM((HEADS * TOK, HEAD), f32),
            pltpu.VMEM((HEADS * TOK, HEAD), f32),
            pltpu.VMEM((HEADS * TOK, HEAD), f32),
            pltpu.VMEM((NY, TOK, 512), bf16),
            pltpu.VMEM((NY, 2, 4, TOK, HEAD), bf16),
            pltpu.VMEM((NY, 3, 2, TOK, HEAD), bf16),
            pltpu.VMEM((NY, 2, TOK, HEAD), bf16),
            pltpu.VMEM((2, NY, TOK, HEAD), bf16),
            dma((6,)),
            dma((4, 2, 4, 4)),
            dma((3, 3)),
            dma((4, NZ)),
            dma((4, NZ, NY)),
            dma((4, NZ)),
            dma((7,)),
            dma((8,)),
            dma((3,)),
            dma((NY,)),
            dma((NY, 3)),
            dma((NY, 3)),
            dma((NY, 2)),
            dma((2, NY)),
        ],
        compiler_params=pltpu.CompilerParams(
            collective_id=0, has_side_effects=True
        ),
    )(tokens, w_query, key_matrix, value_matrix, w_out.T, table)


def solution(mesh):
    in_specs = (
        P("ctx", "fsdp"),
        P("ctx", "fsdp"),
        P("ctx", "fsdp"),
        P("ctx", "fsdp"),
        P("fsdp", "ctx"),
    )
    out_specs = P("ctx", "fsdp")
    return jax.shard_map(body, mesh=mesh, in_specs=in_specs, out_specs=out_specs, check_vma=False)
```

```python
import functools
import math

import jax
import jax.numpy as jnp
import numpy as np
from jax import lax
from jax.experimental import pallas as pl
from jax.experimental.pallas import tpu as pltpu
from jax.sharding import PartitionSpec as P

MESH = pl.DeviceIdType.MESH
HEAD = 128
HEADS = 4
NZ, NY = 8, 4
TOK = 128
SCALE2 = math.log2(math.e) / math.sqrt(HEAD)
REACH = ((4, 3), (3, 4))
WKV, WQ, KV, WO, WB = 0, 1, 2, 3, 4
FIRST = 48


def kernel(
    tok, wq, wk, wv, wo, invf, out,
    xbuf, wkvbuf, wqbuf, kvbuf, wobuf, table, qbuf, proj, mbuf, lbuf, acc, abuf, pbuf, rbuf, sbuf, ybuf,
    local, zsend, ysend, bsend, zrecv, yrecv, brecv, orecv, tsend, trecv, lsend, lrecv, asend, arecv, rsend, rrecv, hsend, hrecv,
):
    c = lax.axis_index("ctx")
    f = lax.axis_index("fsdp")
    k = c % 2
    y = (c // 2) % NY
    z = c // (2 * NY)
    x = f % 4
    yh = f // 4

    def at(zz, yy, kk):
        return ((zz * NY + yy) * 2 + kk, f)

    def up(d, n):
        return (z + (n if d == 0 else NZ - n)) % NZ

    near = (y, y + 1 - 2 * (y % 2), 2 - y // 2, 3 - 3 * (y // 2))
    bufs = (wkvbuf, wqbuf, kvbuf)

    base = (2 * (y // 2), 2 - 2 * (y // 2))

    def remote(ref, send, recv, peer):
        return pltpu.make_async_remote_copy(
            src_ref=ref, dst_ref=ref, send_sem=send, recv_sem=recv, device_id=peer, device_id_type=MESH
        )

    def view(g, zz, yy, kk):
        if g == WQ:
            return wqbuf.at[zz, yy, kk, pl.ds(0, FIRST)]
        return bufs[g].at[zz, yy, kk]

    def late(zz, yy, kk):
        return wqbuf.at[zz, yy, kk, pl.ds(FIRST, 64 - FIRST)]

    def pair(g, zz, p):
        if g == WO:
            return wobuf.at[zz, k]
        if g == WB:
            return late(zz, y, k)
        return view(g, zz, pl.ds(base[p], 2), k)

    def recv_of(g, zz, p):
        return orecv.at[g - WO, zz] if g >= WO else zrecv.at[g, zz, p]

    def zcopy(g, d, step, p):
        zz = up(1 - d, step)
        return remote(pair(g, zz, p), zsend.at[g], recv_of(g, zz, p), at(up(d, 1), y, k))

    def zfirst(g, d, n):
        return remote(view(g, z, near[n], k), zsend.at[g], zrecv.at[g, z, 0], at(up(d, 1), y, k))

    def ycopy(g, n):
        return remote(view(g, z, y, k), ysend.at[g], yrecv.at[g, min(n, 2) - 1], at(z, near[n], k))

    sibling = at(z, y, 1 - k)

    def bcopy(g, zz, kk):
        ref = wobuf.at[:, kk] if g == WO else late(slice(None), slice(None), kk) if g == WB else view(g, zz, slice(None), kk)
        return remote(ref, bsend.at[g], brecv.at[g, zz], sibling)

    def paired(g, zz):
        bcopy(g, zz, 1 - k).wait_recv()

    def open_y(g):
        for n in (1, 2, 3):
            ycopy(g, n).start()

    def open_z(g):
        for d in (0, 1):
            if g >= WO:
                zcopy(g, d, 0, 0).start()
            else:
                zfirst(g, d, 0).start()

    def step0a(g):
        remote(view(g, z, near[1], k), ysend.at[g], yrecv.at[g, 0], sibling).wait_recv()
        for d in (0, 1):
            zfirst(g, d, 1).start()

    def step0b(g):
        remote(pair(g, z, 1), ysend.at[g], yrecv.at[g, 1], sibling).wait_recv()
        for d in (0, 1):
            zcopy(g, d, 0, 1).start()
        bcopy(g, z, k).start()

    def step(g, s):
        for p in (0, 1):
            for d in (0, 1):
                if s <= REACH[d][p] and (g < WO or p == 0):
                    zz = up(1 - d, s)
                    remote(pair(g, zz, p), zsend.at[g], recv_of(g, zz, p), sibling).wait_recv()
                    if s < REACH[d][p]:
                        zcopy(g, d, s, p).start()
        if g < WO:
            bcopy(g, up(1, s), k).start()
            if s < 4:
                bcopy(g, up(0, s), k).start()
        elif s == 4 and g == WO:
            bcopy(g, 0, k).start()

    def wcopy(n, yy):
        return remote(late(slice(None), yy, k), lsend.at[0], lrecv.at[yy], at(z, near[n], k))

    def drain(g):
        if g == WO:
            remote(wobuf.at[pl.ds(0, 7), k], zsend.at[g], orecv.at[0, 0], sibling).wait_send()
            bcopy(g, 0, k).wait_send()
            return
        if g == WB:
            remote(late(pl.ds(0, 7), y, k), zsend.at[g], orecv.at[0, 0], sibling).wait_send()
            remote(late(slice(None), pl.ds(0, 3), k), lsend.at[0], orecv.at[0, 0], sibling).wait_send()
            bcopy(g, 0, k).wait_send()
            return
        remote(view(g, pl.ds(0, 7), slice(None), k), zsend.at[g], orecv.at[0, 0], sibling).wait_send()
        remote(view(g, 0, pl.ds(0, 3), k), ysend.at[g], orecv.at[0, 0], sibling).wait_send()
        remote(view(g, slice(None), slice(None), k), bsend.at[g], orecv.at[0, 0], sibling).wait_send()

    def tcopy(slot, peer):
        return remote(xbuf.at[slot], tsend.at[0], trecv.at[slot], (c, peer))

    def tok_arrived(slot):
        tcopy(slot, yh * 4 + (x + 1) % 4).wait_recv()

    other = 1 - yh
    xr = yh * 4 + (x + 1) % 4
    xl = yh * 4 + (x + 3) % 4
    twin = other * 4 + x
    twin_l = other * 4 + (x + 3) % 4
    twin_r = other * 4 + (x + 1) % 4
    tokens_out = (
        (f, twin), (f, xr), (f, xl),
        (xl, xr),
        (twin, xr), (twin, xl),
        (twin_r, xl),
    )

    mine = wkvbuf.at[z, y, k]
    copies = [
        pltpu.make_async_copy(wk, mine.at[:, pl.ds(0, HEAD)], local.at[0]),
        pltpu.make_async_copy(wv, mine.at[:, pl.ds(HEAD, HEAD)], local.at[1]),
        pltpu.make_async_copy(wo, wobuf.at[z, k], local.at[2]),
        pltpu.make_async_copy(wq, wqbuf.at[z, y, k], local.at[3]),
        pltpu.make_async_copy(tok, xbuf.at[f], local.at[4]),
        pltpu.make_async_copy(invf, table, local.at[5]),
    ]
    for copy in copies:
        copy.start()

    barrier = pltpu.get_barrier_semaphore()
    peers = [at(up(0, 1), y, k), at(up(1, 1), y, k), at(z, y, 1 - k)]
    peers += [at(z, near[n], k) for n in (1, 2, 3)]
    peers += [(c, yh * 4 + (x + dx) % 4) for dx in (1, 2, 3)]
    peers += [((z * NY + near[n]) * 2 + k, twin) for n in (0, 1, 2, 3)]
    for peer in peers:
        pl.semaphore_signal(barrier, inc=1, device_id=peer, device_id_type=MESH)
    for copy in copies:
        copy.wait()
    pl.semaphore_wait(barrier, len(peers))

    open_z(WKV)
    open_y(WKV)
    open_z(WB)
    open_z(WO)
    open_z(WQ)
    open_y(WQ)
    tcopy(*tokens_out[1]).start()
    tcopy(*tokens_out[2]).start()
    step0a(WKV)
    step(WB, 1)
    step(WO, 1)
    step0a(WQ)
    step0b(WKV)
    step(WB, 2)
    step(WKV, 1)
    step(WO, 2)
    step0b(WQ)
    tcopy(*tokens_out[0]).start()
    step(WB, 3)
    step(WKV, 2)
    step(WO, 3)
    tok_arrived(xl)
    tcopy(*tokens_out[3]).start()
    tok_arrived(xr)
    step(WB, 4)
    for n in (1, 2, 3):
        wcopy(n, y).start()
    step(WKV, 3)
    step(WO, 4)
    step(WQ, 1)
    tok_arrived(twin)
    tcopy(*tokens_out[4]).start()
    tcopy(*tokens_out[5]).start()
    step(WKV, 4)

    position = (c * TOK + lax.broadcasted_iota(jnp.int32, (TOK, HEAD), 0)).astype(jnp.float32)
    angle = position * table[...]
    cosine = jnp.cos(angle)
    lane = lax.broadcasted_iota(jnp.int32, (TOK, HEAD), 1)
    sine = jnp.sin(angle) * jnp.where(lane < HEAD // 2, -1.0, 1.0).astype(jnp.float32)

    def turned(piece):
        return (piece * cosine + pltpu.roll(piece, HEAD // 2, 1) * sine).astype(jnp.bfloat16)

    tok_arrived(twin_r)
    tcopy(*tokens_out[6]).start()
    step(WQ, 2)
    tok_arrived(twin_l)
    tok_arrived(yh * 4 + (x + 2) % 4)
    tok_arrived(other * 4 + (x + 2) % 4)

    for s in range(NZ):
        paired(WKV, up(0, s))
    both = jnp.zeros((TOK, 2 * HEAD), jnp.float32)
    for s in range(NZ):
        both += jnp.dot(xbuf[s], wkvbuf[s].reshape(512, 2 * HEAD), preferred_element_type=jnp.float32)
    kvbuf[z, y, k, 0] = turned(both[:, :HEAD])
    kvbuf[z, y, k, 1] = both[:, HEAD:].astype(jnp.bfloat16)
    open_z(KV)
    open_y(KV)

    def multiply(zz, first=False):
        paired(WQ, zz)
        term = jnp.dot(xbuf[zz], wqbuf[zz].reshape(512, 512), preferred_element_type=jnp.float32)
        proj[...] = term if first else proj[...] + term

    step(WQ, 3)
    for n in (1, 2, 3):
        wcopy(n, near[n]).wait_recv()
    bcopy(WB, 0, k).start()
    step0a(KV)
    step0b(KV)
    bcopy(WB, 0, 1 - k).wait_recv()
    multiply(z, True)
    multiply(up(1, 1))
    multiply(up(0, 1))
    multiply(up(1, 2))
    multiply(up(0, 2))
    step(WQ, 4)
    step(KV, 1)
    multiply(up(1, 3))
    multiply(up(0, 3))
    multiply(up(0, 4))
    for h in range(HEADS):
        qbuf[pl.ds(h * TOK, TOK), :] = turned(proj[:, pl.ds(h * HEAD, HEAD)])

    rows = 256
    keys = NY * 2 * TOK

    def attend(zz, first=False):
        paired(KV, zz)

        def some():
            def body(i, carry):
                at_rows = pl.ds(pl.multiple_of(i * rows, rows), rows)
                key = kvbuf[zz, :, :, 0].reshape(keys, HEAD)
                value = kvbuf[zz, :, :, 1].reshape(keys, HEAD)
                score = lax.dot_general(
                    qbuf[at_rows, :], key, (((1,), (1,)), ((), ())), preferred_element_type=jnp.float32
                )
                if first:
                    key_at = lax.broadcasted_iota(jnp.int32, (rows, keys), 1)
                    query_at = (y * 2 + k) * TOK + lax.broadcasted_iota(jnp.int32, (rows, keys), 0) % TOK
                    score = jnp.where(key_at <= query_at, score, jnp.float32(-1e30))
                top = jnp.max(score, axis=1, keepdims=True)
                if first:
                    new = jnp.broadcast_to(top, (rows, HEAD))
                else:
                    old = mbuf[at_rows, :]
                    new = jnp.maximum(old, top)
                exps = jnp.exp2(score * SCALE2 - jnp.tile(new * SCALE2, (1, keys // HEAD)))
                total = jnp.sum(exps, axis=1, keepdims=True)
                summed = jnp.dot(exps.astype(jnp.bfloat16), value, preferred_element_type=jnp.float32)
                if first:
                    lbuf[at_rows, :] = jnp.broadcast_to(total, (rows, HEAD))
                    acc[at_rows, :] = summed
                else:
                    factor = jnp.exp2((old - new) * SCALE2)
                    lbuf[at_rows, :] = lbuf[at_rows, :] * factor + total
                    acc[at_rows, :] = acc[at_rows, :] * factor + summed
                mbuf[at_rows, :] = new
                return carry

            lax.fori_loop(0, HEADS * TOK // rows, body, 0)

        if first:
            some()
        else:
            pl.when(zz <= z)(some)

    inner = jnp.logical_or(y == 1, y == 2)

    def acopy(kind, n, yy):
        return remote(abuf.at[yy], asend.at[kind], arecv.at[yy], at(z, near[n], k))

    def finish():
        for h in range(HEADS):
            at_rows = pl.ds(h * TOK, TOK)
            abuf[y, :, pl.ds(h * HEAD, HEAD)] = (acc[at_rows, :] / lbuf[at_rows, :]).astype(jnp.bfloat16)
        acopy(0, 1, y).start()
        pl.when(inner)(lambda: acopy(1, 2, y).start())

    attend(z, True)
    pl.when(z == 0)(finish)
    step(KV, 2)
    attend(up(1, 1))
    attend(up(0, 1))
    pl.when(z == 1)(finish)
    step(KV, 3)
    attend(up(1, 2))
    attend(up(0, 2))
    pl.when(z == 2)(finish)
    step(KV, 4)
    attend(up(1, 3))
    attend(up(0, 3))
    attend(up(0, 4))
    pl.when(z >= 3)(finish)

    bcopy(WO, 0, 1 - k).wait_recv()

    def rcopy(n, dx):
        there = (x + dx) % 4
        return pltpu.make_async_remote_copy(
            src_ref=pbuf.at[n, :, there], dst_ref=rbuf.at[n, dx - 1], send_sem=rsend.at[0],
            recv_sem=rrecv.at[n], device_id=(c, yh * 4 + there), device_id_type=MESH,
        )

    def pass_on(n):
        acopy(0, 1, near[n]).wait_recv()
        pl.when(inner)(lambda: acopy(1 + n, 2 if n == 1 else 1, near[n]).start())

    def make_terms(n):
        terms = lax.dot_general(
            abuf[near[n]], wobuf[...].reshape(1024, 512), (((1,), (1,)), ((), ())),
            preferred_element_type=jnp.float32,
        ).astype(jnp.bfloat16)
        for slot in range(8):
            pbuf[n, slot // 4, slot % 4] = terms[:, slot * HEAD:(slot + 1) * HEAD]
        for dx in (2, 1, 3):
            rcopy(n, dx).start()

    def hcopy(n, j):
        half = (other, yh)[j]
        return pltpu.make_async_remote_copy(
            src_ref=sbuf.at[n, j], dst_ref=ybuf.at[yh * 4 + y], send_sem=hsend.at[0], recv_sem=hrecv.at[0],
            device_id=((z * NY + near[n]) * 2 + k, half * 4 + x), device_id_type=MESH,
        )

    def sum_over_x(n):
        remote(rbuf.at[n], rsend.at[0], rrecv.at[n], sibling).wait_recv()
        for j, half in ((0, other), (1, yh)):
            total = pbuf[n, half, x].astype(jnp.float32)
            for dx in (1, 2, 3):
                total = total + rbuf[n, dx - 1, half].astype(jnp.float32)
            if n == 0 and j == 1:
                ybuf[yh * 4 + y] = total.astype(jnp.bfloat16)
            else:
                sbuf[n, j] = total.astype(jnp.bfloat16)
                hcopy(n, j).start()

    make_terms(0)
    pass_on(1)
    make_terms(1)
    pass_on(2)
    make_terms(2)
    sum_over_x(0)
    pass_on(3)
    make_terms(3)
    sum_over_x(1)
    sum_over_x(2)
    sum_over_x(3)
    for g in (WKV, WQ, KV, WO, WB):
        drain(g)
    remote(xbuf.at[pl.ds(0, 7)], tsend.at[0], orecv.at[0, 0], sibling).wait_send()
    acopy(0, 1, y).wait_send()

    @pl.when(inner)
    def _():
        for kind in (1, 2, 3, 4):
            acopy(kind, 1, y).wait_send()

    remote(rbuf, rsend.at[0], orecv.at[0, 0], sibling).wait_send()
    remote(ybuf.at[pl.ds(0, 7)], hsend.at[0], hrecv.at[0], sibling).wait_send()
    remote(ybuf.at[pl.ds(0, 7)], hsend.at[0], hrecv.at[0], sibling).wait_recv()
    for n in range(NY):
        out[:, pl.ds(n * HEAD, HEAD)] = (
            ybuf[n].astype(jnp.float32) + ybuf[4 + n].astype(jnp.float32)
        ).astype(jnp.bfloat16)


def body(tokens, w_query, key_matrix, value_matrix, w_out):
    half = HEAD // 2
    inverse_freq = np.power(
        np.float32(500000.0), -np.arange(half, dtype=np.float32) * np.float32(2.0) / np.float32(HEAD)
    ).astype(np.float32)
    table = jnp.asarray(np.concatenate([inverse_freq, inverse_freq])[None, :])
    hbm = pl.BlockSpec(memory_space=pltpu.HBM)
    vmem = pl.BlockSpec(memory_space=pltpu.VMEM)
    bf16, f32 = jnp.bfloat16, jnp.float32
    dma = pltpu.SemaphoreType.DMA
    return pl.pallas_call(
        kernel,
        out_shape=jax.ShapeDtypeStruct((TOK, 512), bf16),
        in_specs=[hbm] * 6,
        out_specs=vmem,
        scratch_shapes=[
            pltpu.VMEM((8, TOK, 512), bf16),
            pltpu.VMEM((NZ, NY, 2, 64, 2 * HEAD), bf16),
            pltpu.VMEM((NZ, NY, 2, 64, 512), bf16),
            pltpu.VMEM((NZ, NY, 2, 2, TOK, HEAD), bf16),
            pltpu.VMEM((NZ, 2, 64, 512), bf16),
            pltpu.VMEM((1, HEAD), f32),
            pltpu.VMEM((HEADS * TOK, HEAD), bf16),
            pltpu.VMEM((TOK, 512), f32),
            pltpu.VMEM((HEADS * TOK, HEAD), f32),
            pltpu.VMEM((HEADS * TOK, HEAD), f32),
            pltpu.VMEM((HEADS * TOK, HEAD), f32),
            pltpu.VMEM((NY, TOK, 512), bf16),
            pltpu.VMEM((NY, 2, 4, TOK, HEAD), bf16),
            pltpu.VMEM((NY, 3, 2, TOK, HEAD), bf16),
            pltpu.VMEM((NY, 2, TOK, HEAD), bf16),
            pltpu.VMEM((2 * NY, TOK, HEAD), bf16),
            dma((6,)),
            dma((5,)),
            dma((3,)),
            dma((5,)),
            dma((3, NZ, 2)),
            dma((3, 2)),
            dma((5, NZ)),
            dma((2, NZ)),
            dma((1,)),
            dma((8,)),
            dma((1,)),
            dma((NY,)),
            dma((5,)),
            dma((NY,)),
            dma((1,)),
            dma((NY,)),
            dma((1,)),
            dma((1,)),
        ],
        compiler_params=pltpu.CompilerParams(
            collective_id=0, has_side_effects=True
        ),
    )(tokens, w_query, key_matrix, value_matrix, w_out.T, table)


def solution(mesh):
    in_specs = (
        P("ctx", "fsdp"),
        P("ctx", "fsdp"),
        P("ctx", "fsdp"),
        P("ctx", "fsdp"),
        P("fsdp", "ctx"),
    )
    out_specs = P("ctx", "fsdp")
    return jax.shard_map(body, mesh=mesh, in_specs=in_specs, out_specs=out_specs, check_vma=False)
```

```python
import functools
import math

import jax
import jax.numpy as jnp
import numpy as np
from jax import lax
from jax.experimental import pallas as pl
from jax.experimental.pallas import tpu as pltpu
from jax.sharding import PartitionSpec as P

MESH = pl.DeviceIdType.MESH
HEAD = 128
HEADS = 4
NZ, NY = 8, 4
TOK = 128
HALF = TOK // 2
SCALE2 = math.log2(math.e) / math.sqrt(HEAD)
REACH = ((4, 3), (3, 4))
WKV, WQ, KV, WO, WB = 0, 1, 2, 3, 4
FIRST = 48


def kernel(
    tok, wq, wk, wv, wo, invf, out,
    xbuf, wkvbuf, wqbuf, kvbuf, wobuf, table, qbuf, proj, mbuf, lbuf, acc, abuf, pbuf, rbuf, sbuf, ybuf,
    local, zsend, ysend, bsend, zrecv, yrecv, brecv, orecv, tsend, trecv, lsend, lrecv, asend, arecv, rsend, rrecv, hsend, hrecv,
):
    c = lax.axis_index("ctx")
    f = lax.axis_index("fsdp")
    k = c % 2
    y = (c // 2) % NY
    z = c // (2 * NY)
    x = f % 4
    yh = f // 4

    def at(zz, yy, kk):
        return ((zz * NY + yy) * 2 + kk, f)

    def up(d, n):
        return (z + (n if d == 0 else NZ - n)) % NZ

    near = (y, y + 1 - 2 * (y % 2), 2 - y // 2, 3 - 3 * (y // 2))
    bufs = (wkvbuf, wqbuf, kvbuf)

    base = (2 * (y // 2), 2 - 2 * (y // 2))

    def remote(ref, send, recv, peer):
        return pltpu.make_async_remote_copy(
            src_ref=ref, dst_ref=ref, send_sem=send, recv_sem=recv, device_id=peer, device_id_type=MESH
        )

    def view(g, zz, yy, kk):
        if g == WQ:
            return wqbuf.at[zz, yy, kk, pl.ds(0, FIRST)]
        return bufs[g].at[zz, yy, kk]

    def late(zz, yy, kk):
        return wqbuf.at[zz, yy, kk, pl.ds(FIRST, 64 - FIRST)]

    def pair(g, zz, p):
        if g == WO:
            return wobuf.at[zz, k]
        if g == WB:
            return late(zz, y, k)
        return view(g, zz, pl.ds(base[p], 2), k)

    def recv_of(g, zz, p):
        return orecv.at[g - WO, zz] if g >= WO else zrecv.at[g, zz, p]

    def zcopy(g, d, step, p):
        zz = up(1 - d, step)
        return remote(pair(g, zz, p), zsend.at[g], recv_of(g, zz, p), at(up(d, 1), y, k))

    def zfirst(g, d, n):
        return remote(view(g, z, near[n], k), zsend.at[g], zrecv.at[g, z, 0], at(up(d, 1), y, k))

    def ycopy(g, n):
        return remote(view(g, z, y, k), ysend.at[g], yrecv.at[g, min(n, 2) - 1], at(z, near[n], k))

    sibling = at(z, y, 1 - k)

    def bcopy(g, zz, kk):
        ref = wobuf.at[:, kk] if g == WO else late(slice(None), slice(None), kk) if g == WB else view(g, zz, slice(None), kk)
        return remote(ref, bsend.at[g], brecv.at[g, zz], sibling)

    def paired(g, zz):
        bcopy(g, zz, 1 - k).wait_recv()

    def open_y(g):
        for n in (1, 2, 3):
            ycopy(g, n).start()

    def open_z(g):
        for d in (0, 1):
            if g >= WO:
                zcopy(g, d, 0, 0).start()
            else:
                zfirst(g, d, 0).start()

    def step0a(g, last):
        remote(view(g, z, near[1], k), ysend.at[g], yrecv.at[g, 0], sibling).wait_recv()
        for d in (0, 1):
            zfirst(g, d, 1).start()
        if last:
            bcopy(g, z, k).start()

    def step0b(g, last):
        remote(pair(g, z, 1), ysend.at[g], yrecv.at[g, 1], sibling).wait_recv()
        for d in (0, 1):
            zcopy(g, d, 0, 1).start()
        if last:
            bcopy(g, z, k).start()

    def step(g, s, p, last):
        for d in (0, 1):
            if s <= REACH[d][p]:
                zz = up(1 - d, s)
                remote(pair(g, zz, p), zsend.at[g], recv_of(g, zz, p), sibling).wait_recv()
                if s < REACH[d][p]:
                    zcopy(g, d, s, p).start()
        if g < WO and last:
            bcopy(g, up(1, s), k).start()
            if s < 4:
                bcopy(g, up(0, s), k).start()
        elif s == 4 and g == WO:
            bcopy(g, 0, k).start()

    def wcopy(n, yy):
        return remote(late(slice(None), yy, k), lsend.at[0], lrecv.at[yy], at(z, near[n], k))

    def drain(g):
        if g == WO:
            remote(wobuf.at[pl.ds(0, 7), k], zsend.at[g], orecv.at[0, 0], sibling).wait_send()
            bcopy(g, 0, k).wait_send()
            return
        if g == WB:
            remote(late(pl.ds(0, 7), y, k), zsend.at[g], orecv.at[0, 0], sibling).wait_send()
            remote(late(slice(None), pl.ds(0, 3), k), lsend.at[0], orecv.at[0, 0], sibling).wait_send()
            bcopy(g, 0, k).wait_send()
            return
        remote(view(g, pl.ds(0, 7), slice(None), k), zsend.at[g], orecv.at[0, 0], sibling).wait_send()
        remote(view(g, 0, pl.ds(0, 3), k), ysend.at[g], orecv.at[0, 0], sibling).wait_send()
        remote(view(g, slice(None), slice(None), k), bsend.at[g], orecv.at[0, 0], sibling).wait_send()

    def tcopy(slot, peer):
        return remote(xbuf.at[slot], tsend.at[0], trecv.at[slot], (c, peer))

    def tok_arrived(slot):
        tcopy(slot, yh * 4 + (x + 1) % 4).wait_recv()

    other = 1 - yh
    xr = yh * 4 + (x + 1) % 4
    xl = yh * 4 + (x + 3) % 4
    twin = other * 4 + x
    twin_l = other * 4 + (x + 3) % 4
    twin_r = other * 4 + (x + 1) % 4
    tokens_out = (
        (f, twin), (f, xr), (f, xl),
        (xl, xr),
        (twin, xr), (twin, xl),
        (twin_r, xl),
    )

    mine = wkvbuf.at[z, y, k]
    copies = [
        pltpu.make_async_copy(wk, mine.at[:, pl.ds(0, HEAD)], local.at[0]),
        pltpu.make_async_copy(wv, mine.at[:, pl.ds(HEAD, HEAD)], local.at[1]),
        pltpu.make_async_copy(wo, wobuf.at[z, k], local.at[2]),
        pltpu.make_async_copy(wq, wqbuf.at[z, y, k], local.at[3]),
        pltpu.make_async_copy(tok, xbuf.at[f], local.at[4]),
        pltpu.make_async_copy(invf, table, local.at[5]),
    ]
    for copy in copies:
        copy.start()

    barrier = pltpu.get_barrier_semaphore()
    peers = [at(up(0, 1), y, k), at(up(1, 1), y, k), at(z, y, 1 - k)]
    peers += [at(z, near[n], k) for n in (1, 2, 3)]
    peers += [(c, yh * 4 + (x + dx) % 4) for dx in (1, 2, 3)]
    peers += [((z * NY + near[n]) * 2 + k, twin) for n in (0, 1, 2, 3)]
    for peer in peers:
        pl.semaphore_signal(barrier, inc=1, device_id=peer, device_id_type=MESH)
    for copy in copies:
        copy.wait()
    pl.semaphore_wait(barrier, len(peers))

    open_z(WKV)
    open_y(WKV)
    open_z(WB)
    open_z(WO)
    open_z(WQ)
    open_y(WQ)
    tcopy(*tokens_out[1]).start()
    tcopy(*tokens_out[2]).start()

    position = (c * TOK + lax.broadcasted_iota(jnp.int32, (TOK, HEAD), 0)).astype(jnp.float32)
    angle = position * table[...]
    cosine = jnp.cos(angle)
    lane = lax.broadcasted_iota(jnp.int32, (TOK, HEAD), 1)
    sine = jnp.sin(angle) * jnp.where(lane < HEAD // 2, -1.0, 1.0).astype(jnp.float32)

    def turned(piece):
        return (piece * cosine + pltpu.roll(piece, HEAD // 2, 1) * sine).astype(jnp.bfloat16)

    def send_late():
        for n in (1, 2, 3):
            wcopy(n, y).start()

    def take_late():
        for n in (1, 2, 3):
            wcopy(n, near[n]).wait_recv()
        bcopy(WB, 0, k).start()

    def make_keys():
        tok_arrived(twin_l)
        tok_arrived(yh * 4 + (x + 2) % 4)
        tok_arrived(other * 4 + (x + 2) % 4)
        for s in range(NZ):
            paired(WKV, up(0, s))
        both = jnp.zeros((TOK, 2 * HEAD), jnp.float32)
        for s in range(NZ):
            both += jnp.dot(xbuf[s], wkvbuf[s].reshape(512, 2 * HEAD), preferred_element_type=jnp.float32)
        kvbuf[z, y, k, 0] = turned(both[:, :HEAD])
        kvbuf[z, y, k, 1] = both[:, HEAD:].astype(jnp.bfloat16)
        open_z(KV)
        open_y(KV)

    def make_queries():
        bcopy(WB, 0, 1 - k).wait_recv()
        for n in range(NZ):
            zz = up(n % 2, (n + 1) // 2)
            paired(WQ, zz)
            term = jnp.dot(xbuf[zz], wqbuf[zz].reshape(512, 512), preferred_element_type=jnp.float32)
            proj[...] = term if n == 0 else proj[...] + term
        for h in range(HEADS):
            qbuf[pl.ds(h * TOK, TOK), :] = turned(proj[:, pl.ds(h * HEAD, HEAD)])

    rows = 256
    keys = NY * 2 * TOK

    def attend(zz, first=False):
        paired(KV, zz)

        def some():
            def body(i, carry):
                at_rows = pl.ds(pl.multiple_of(i * rows, rows), rows)
                key = kvbuf[zz, :, :, 0].reshape(keys, HEAD)
                value = kvbuf[zz, :, :, 1].reshape(keys, HEAD)
                score = lax.dot_general(
                    qbuf[at_rows, :], key, (((1,), (1,)), ((), ())), preferred_element_type=jnp.float32
                )
                if first:
                    key_at = lax.broadcasted_iota(jnp.int32, (rows, keys), 1)
                    query_at = (y * 2 + k) * TOK + lax.broadcasted_iota(jnp.int32, (rows, keys), 0) % TOK
                    score = jnp.where(key_at <= query_at, score, jnp.float32(-1e30))
                top = jnp.max(score, axis=1, keepdims=True)
                if first:
                    new = jnp.broadcast_to(top, (rows, HEAD))
                else:
                    old = mbuf[at_rows, :]
                    new = jnp.maximum(old, top)
                exps = jnp.exp2(score * SCALE2 - jnp.tile(new * SCALE2, (1, keys // HEAD)))
                total = jnp.sum(exps, axis=1, keepdims=True)
                summed = jnp.dot(exps.astype(jnp.bfloat16), value, preferred_element_type=jnp.float32)
                if first:
                    lbuf[at_rows, :] = jnp.broadcast_to(total, (rows, HEAD))
                    acc[at_rows, :] = summed
                else:
                    factor = jnp.exp2((old - new) * SCALE2)
                    lbuf[at_rows, :] = lbuf[at_rows, :] * factor + total
                    acc[at_rows, :] = acc[at_rows, :] * factor + summed
                mbuf[at_rows, :] = new
                return carry

            lax.fori_loop(0, HEADS * TOK // rows, body, 0)

        if first:
            some()
        else:
            pl.when(zz <= z)(some)

    inner = jnp.logical_or(y == 1, y == 2)

    def acopy(kind, n, yy, h):
        ref = abuf.at[yy, pl.ds(h * HALF, HALF)]
        return remote(ref, asend.at[kind], arecv.at[yy, h], at(z, near[n], k))

    def finish():
        for h in range(HEADS):
            at_rows = pl.ds(h * TOK, TOK)
            abuf[y, :, pl.ds(h * HEAD, HEAD)] = (acc[at_rows, :] / lbuf[at_rows, :]).astype(jnp.bfloat16)
        for h in (0, 1):
            acopy(0, 1, y, h).start()

            @pl.when(inner)
            def _():
                acopy(1, 2, y, h).start()

    step0a(WKV, False)
    step(WB, 1, 0, True)
    step(WO, 1, 0, True)
    step0a(WQ, False)
    step0b(WKV, True)
    step(WB, 2, 0, True)
    step(WKV, 1, 0, False)
    step(WKV, 1, 1, True)
    step(WO, 2, 0, True)
    step0b(WQ, True)
    tcopy(*tokens_out[0]).start()
    step(WB, 3, 0, True)
    step(WKV, 2, 0, False)
    step(WKV, 2, 1, True)
    step(WO, 3, 0, True)
    tok_arrived(xl)
    tcopy(*tokens_out[3]).start()
    tok_arrived(xr)
    step(WB, 4, 0, True)
    send_late()
    step(WKV, 3, 0, False)
    step(WKV, 3, 1, True)
    step(WO, 4, 0, True)
    step(WQ, 1, 0, False)
    step(WQ, 1, 1, True)
    tok_arrived(twin)
    tcopy(*tokens_out[4]).start()
    tcopy(*tokens_out[5]).start()
    step(WKV, 4, 0, False)
    step(WKV, 4, 1, True)
    tok_arrived(twin_r)
    tcopy(*tokens_out[6]).start()
    step(WQ, 2, 0, False)
    step(WQ, 2, 1, True)
    make_keys()
    step(WQ, 3, 0, False)
    step(WQ, 3, 1, True)
    take_late()
    step0a(KV, False)
    step0b(KV, True)
    step(WQ, 4, 0, False)
    step(WQ, 4, 1, True)
    step(KV, 1, 0, False)
    step(KV, 1, 1, True)
    make_queries()
    attend(z, True)
    pl.when(z == 0)(finish)
    step(KV, 2, 0, False)
    step(KV, 2, 1, True)
    attend(up(1, 1))
    attend(up(0, 1))
    pl.when(z == 1)(finish)
    step(KV, 3, 0, False)
    step(KV, 3, 1, True)
    attend(up(1, 2))
    attend(up(0, 2))
    pl.when(z == 2)(finish)
    step(KV, 4, 0, False)
    step(KV, 4, 1, True)
    attend(up(1, 3))
    attend(up(0, 3))
    attend(up(1, 4))
    pl.when(z >= 3)(finish)

    bcopy(WO, 0, 1 - k).wait_recv()

    def rcopy(n, h, dx):
        there = (x + dx) % 4
        return pltpu.make_async_remote_copy(
            src_ref=pbuf.at[n, h, :, there], dst_ref=rbuf.at[n, h, dx - 1], send_sem=rsend.at[0],
            recv_sem=rrecv.at[n, h], device_id=(c, yh * 4 + there), device_id_type=MESH,
        )

    def pass_on(n, h):
        acopy(0, 1, near[n], h).wait_recv()

        @pl.when(inner)
        def _():
            acopy(1 + n, 2 if n == 1 else 1, near[n], h).start()

    def make_terms(n, h):
        terms = lax.dot_general(
            abuf[near[n], pl.ds(h * HALF, HALF), :], wobuf[...].reshape(1024, 512), (((1,), (1,)), ((), ())),
            preferred_element_type=jnp.float32,
        ).astype(jnp.bfloat16)
        for slot in range(8):
            pbuf[n, h, slot // 4, slot % 4] = terms[:, slot * HEAD:(slot + 1) * HEAD]
        for dx in (2, 1, 3):
            rcopy(n, h, dx).start()

    def hcopy(n, h, j):
        half = (other, yh)[j]
        return pltpu.make_async_remote_copy(
            src_ref=sbuf.at[n, h, j], dst_ref=ybuf.at[yh * 4 + y, pl.ds(h * HALF, HALF)], send_sem=hsend.at[0],
            recv_sem=hrecv.at[0], device_id=((z * NY + near[n]) * 2 + k, half * 4 + x), device_id_type=MESH,
        )

    def sum_over_x(n, h):
        remote(rbuf.at[n, h], rsend.at[0], rrecv.at[n, h], sibling).wait_recv()
        for j, half in ((0, other), (1, yh)):
            total = pbuf[n, h, half, x].astype(jnp.float32)
            for dx in (1, 2, 3):
                total = total + rbuf[n, h, dx - 1, half].astype(jnp.float32)
            if n == 0 and j == 1:
                ybuf[yh * 4 + y, pl.ds(h * HALF, HALF), :] = total.astype(jnp.bfloat16)
            else:
                sbuf[n, h, j] = total.astype(jnp.bfloat16)
                hcopy(n, h, j).start()

    make_terms(0, 0)
    make_terms(0, 1)
    pass_on(1, 0)
    make_terms(1, 0)
    pass_on(2, 0)
    pass_on(1, 1)
    make_terms(1, 1)
    pass_on(2, 1)
    make_terms(2, 0)
    sum_over_x(0, 0)
    pass_on(3, 0)
    make_terms(2, 1)
    sum_over_x(0, 1)
    make_terms(3, 0)
    pass_on(3, 1)
    make_terms(3, 1)
    sum_over_x(1, 0)
    sum_over_x(1, 1)
    sum_over_x(2, 0)
    sum_over_x(2, 1)
    sum_over_x(3, 0)
    sum_over_x(3, 1)
    for g in (WKV, WQ, KV, WO, WB):
        drain(g)
    remote(xbuf.at[pl.ds(0, 7)], tsend.at[0], orecv.at[0, 0], sibling).wait_send()
    remote(abuf.at[y], asend.at[0], orecv.at[0, 0], sibling).wait_send()

    @pl.when(inner)
    def _():
        for kind in (1, 2, 3, 4):
            remote(abuf.at[y], asend.at[kind], orecv.at[0, 0], sibling).wait_send()

    remote(rbuf, rsend.at[0], orecv.at[0, 0], sibling).wait_send()
    remote(ybuf.at[pl.ds(0, 7)], hsend.at[0], hrecv.at[0], sibling).wait_send()
    remote(ybuf.at[pl.ds(0, 7)], hsend.at[0], hrecv.at[0], sibling).wait_recv()
    for n in range(NY):
        out[:, pl.ds(n * HEAD, HEAD)] = (
            ybuf[n].astype(jnp.float32) + ybuf[4 + n].astype(jnp.float32)
        ).astype(jnp.bfloat16)


def body(tokens, w_query, key_matrix, value_matrix, w_out):
    half = HEAD // 2
    inverse_freq = np.power(
        np.float32(500000.0), -np.arange(half, dtype=np.float32) * np.float32(2.0) / np.float32(HEAD)
    ).astype(np.float32)
    table = jnp.asarray(np.concatenate([inverse_freq, inverse_freq])[None, :])
    hbm = pl.BlockSpec(memory_space=pltpu.HBM)
    vmem = pl.BlockSpec(memory_space=pltpu.VMEM)
    bf16, f32 = jnp.bfloat16, jnp.float32
    dma = pltpu.SemaphoreType.DMA
    operands = [
        pltpu.with_memory_space_constraint(a, pltpu.HBM)
        for a in (tokens, w_query, key_matrix, value_matrix, w_out.T, table)
    ]
    return pl.pallas_call(
        kernel,
        out_shape=jax.ShapeDtypeStruct((TOK, 512), bf16),
        in_specs=[hbm] * 6,
        out_specs=vmem,
        scratch_shapes=[
            pltpu.VMEM((8, TOK, 512), bf16),
            pltpu.VMEM((NZ, NY, 2, 64, 2 * HEAD), bf16),
            pltpu.VMEM((NZ, NY, 2, 64, 512), bf16),
            pltpu.VMEM((NZ, NY, 2, 2, TOK, HEAD), bf16),
            pltpu.VMEM((NZ, 2, 64, 512), bf16),
            pltpu.VMEM((1, HEAD), f32),
            pltpu.VMEM((HEADS * TOK, HEAD), bf16),
            pltpu.VMEM((TOK, 512), f32),
            pltpu.VMEM((HEADS * TOK, HEAD), f32),
            pltpu.VMEM((HEADS * TOK, HEAD), f32),
            pltpu.VMEM((HEADS * TOK, HEAD), f32),
            pltpu.VMEM((NY, TOK, 512), bf16),
            pltpu.VMEM((NY, 2, 2, 4, HALF, HEAD), bf16),
            pltpu.VMEM((NY, 2, 3, 2, HALF, HEAD), bf16),
            pltpu.VMEM((NY, 2, 2, HALF, HEAD), bf16),
            pltpu.VMEM((2 * NY, TOK, HEAD), bf16),
            dma((6,)),
            dma((5,)),
            dma((3,)),
            dma((5,)),
            dma((3, NZ, 2)),
            dma((3, 2)),
            dma((5, NZ)),
            dma((2, NZ)),
            dma((1,)),
            dma((8,)),
            dma((1,)),
            dma((NY,)),
            dma((5,)),
            dma((NY, 2)),
            dma((1,)),
            dma((NY, 2)),
            dma((1,)),
            dma((1,)),
        ],
        compiler_params=pltpu.CompilerParams(
            collective_id=0, has_side_effects=True, vmem_limit_bytes=50 * 2**20
        ),
    )(*operands)


def solution(mesh):
    in_specs = (
        P("ctx", "fsdp"),
        P("ctx", "fsdp"),
        P("ctx", "fsdp"),
        P("ctx", "fsdp"),
        P("fsdp", "ctx"),
    )
    out_specs = P("ctx", "fsdp")
    return jax.shard_map(body, mesh=mesh, in_specs=in_specs, out_specs=out_specs, check_vma=False)
```

```python
import functools
import math

import jax
import jax.numpy as jnp
import numpy as np
from jax import lax
from jax.experimental import pallas as pl
from jax.experimental.pallas import tpu as pltpu
from jax.sharding import PartitionSpec as P

MESH = pl.DeviceIdType.MESH
HEAD = 128
HEADS = 4
NZ, NY = 8, 4
TOK = 128
HALF = TOK // 2
SCALE2 = math.log2(math.e) / math.sqrt(HEAD)
REACH = ((4, 3), (3, 4))
WKV, WQ, KV, WO, WB, WP = 0, 1, 2, 3, 4, 5
FIRST = 48


def kernel(
    tok, wq, wk, wv, wo, invf, out,
    xbuf, wkvbuf, wqbuf, kvbuf, wobuf, table, qbuf, proj, mbuf, lbuf, acc, abuf, pbuf, rbuf, sbuf, ybuf,
    local, zsend, ysend, bsend, ksend, zrecv, yrecv, brecv, orecv, tsend, trecv, lsend, lrecv, osend, asend, arecv, rsend, rrecv, hsend, hrecv,
):
    c = lax.axis_index("ctx")
    f = lax.axis_index("fsdp")
    k = c % 2
    y = (c // 2) % NY
    z = c // (2 * NY)
    x = f % 4
    yh = f // 4

    def at(zz, yy, kk):
        return ((zz * NY + yy) * 2 + kk, f)

    def up(d, n):
        return (z + (n if d == 0 else NZ - n)) % NZ

    near = (y, y + 1 - 2 * (y % 2), 2 - y // 2, 3 - 3 * (y // 2))
    bufs = (wkvbuf, wqbuf, kvbuf)

    base = (2 * (y // 2), 2 - 2 * (y // 2))

    def remote(ref, send, recv, peer):
        return pltpu.make_async_remote_copy(
            src_ref=ref, dst_ref=ref, send_sem=send, recv_sem=recv, device_id=peer, device_id_type=MESH
        )

    def view(g, zz, yy, kk):
        if g == WQ:
            return wqbuf.at[zz, yy, kk, pl.ds(0, FIRST)]
        return bufs[g].at[zz, yy, kk]

    def late(zz, yy, kk):
        return wqbuf.at[zz, yy, kk, pl.ds(FIRST, 64 - FIRST)]

    def pair(g, zz, p):
        if g == WO:
            return wobuf.at[0, zz, k]
        if g == WP:
            return wobuf.at[1, zz, k]
        if g == WB:
            return late(zz, y, k)
        return view(g, zz, pl.ds(base[p], 2), k)

    def recv_of(g, zz, p):
        return orecv.at[g - WO, zz] if g >= WO else zrecv.at[g, zz, p]

    def zcopy(g, d, step, p):
        zz = up(1 - d, step)
        return remote(pair(g, zz, p), zsend.at[g], recv_of(g, zz, p), at(up(d, 1), y, k))

    def zfirst(g, d, n):
        return remote(view(g, z, near[n], k), zsend.at[g], zrecv.at[g, z, 0], at(up(d, 1), y, k))

    def ycopy(g, n):
        return remote(view(g, z, y, k), ysend.at[g], yrecv.at[g, min(n, 2) - 1], at(z, near[n], k))

    sibling = at(z, y, 1 - k)

    def bcopy(g, zz, kk):
        ref = wobuf.at[g // WP, :, kk] if g in (WO, WP) else late(slice(None), slice(None), kk) if g == WB else view(g, zz, slice(None), kk)
        return remote(ref, ksend.at[zz] if g == KV else bsend.at[g], brecv.at[g, zz], sibling)

    def share(g, zz):
        if g == KV:
            pl.when(zz <= z)(lambda: bcopy(g, zz, k).start())
        else:
            bcopy(g, zz, k).start()

    def paired(g, zz):
        bcopy(g, zz, 1 - k).wait_recv()

    def open_y(g):
        for n in (1, 2, 3):
            ycopy(g, n).start()

    def open_z(g):
        for d in (0, 1):
            if g >= WO:
                zcopy(g, d, 0, 0).start()
            else:
                zfirst(g, d, 0).start()

    def step0a(g, last):
        remote(view(g, z, near[1], k), ysend.at[g], yrecv.at[g, 0], sibling).wait_recv()
        for d in (0, 1):
            zfirst(g, d, 1).start()
        if last:
            bcopy(g, z, k).start()

    def step0b(g, last):
        remote(pair(g, z, 1), ysend.at[g], yrecv.at[g, 1], sibling).wait_recv()
        for d in (0, 1):
            zcopy(g, d, 0, 1).start()
        if last:
            bcopy(g, z, k).start()

    def step(g, s, p, last):
        for d in (0, 1):
            if s <= REACH[d][p]:
                zz = up(1 - d, s)
                remote(pair(g, zz, p), zsend.at[g], recv_of(g, zz, p), sibling).wait_recv()
                if s < REACH[d][p]:
                    zcopy(g, d, s, p).start()
        if g < WO and last:
            share(g, up(1, s))
            if s < 4:
                share(g, up(0, s))
        elif s == 4 and g in (WO, WP):
            bcopy(g, 0, k).start()

    def wcopy(n, yy):
        return remote(late(slice(None), yy, k), lsend.at[0], lrecv.at[yy], at(z, near[n], k))

    def drain(g):
        if g in (WO, WP):
            remote(wobuf.at[0, pl.ds(0, 7), k], zsend.at[g], orecv.at[0, 0], sibling).wait_send()
            bcopy(g, 0, k).wait_send()
            return
        if g == WB:
            remote(late(pl.ds(0, 7), y, k), zsend.at[g], orecv.at[0, 0], sibling).wait_send()
            remote(late(slice(None), pl.ds(0, 3), k), lsend.at[0], orecv.at[0, 0], sibling).wait_send()
            bcopy(g, 0, k).wait_send()
            return
        remote(view(g, pl.ds(0, 7), slice(None), k), zsend.at[g], orecv.at[0, 0], sibling).wait_send()
        remote(view(g, 0, pl.ds(0, 3), k), ysend.at[g], orecv.at[0, 0], sibling).wait_send()
        if g == KV:
            for zz in range(NZ):
                pl.when(zz <= z)(lambda: bcopy(g, zz, k).wait_send())
        else:
            remote(view(g, slice(None), slice(None), k), bsend.at[g], orecv.at[0, 0], sibling).wait_send()

    def tcopy(slot, peer):
        return remote(xbuf.at[slot], tsend.at[0], trecv.at[slot], (c, peer))

    def tok_arrived(slot):
        tcopy(slot, yh * 4 + (x + 1) % 4).wait_recv()

    other = 1 - yh
    xr = yh * 4 + (x + 1) % 4
    xl = yh * 4 + (x + 3) % 4
    twin = other * 4 + x
    twin_l = other * 4 + (x + 3) % 4
    twin_r = other * 4 + (x + 1) % 4
    tokens_out = (
        (f, twin), (f, xr), (f, xl),
        (xl, xr),
        (twin, xr), (twin, xl),
        (twin_r, xl),
    )

    mine = wkvbuf.at[z, y, k]
    copies = [
        pltpu.make_async_copy(wk, mine.at[:, pl.ds(0, HEAD)], local.at[0]),
        pltpu.make_async_copy(wv, mine.at[:, pl.ds(HEAD, HEAD)], local.at[1]),
        pltpu.make_async_copy(wo, wobuf.at[0, z, k], local.at[2]),
        pltpu.make_async_copy(wq, wqbuf.at[z, y, k], local.at[3]),
        pltpu.make_async_copy(tok, xbuf.at[f], local.at[4]),
        pltpu.make_async_copy(invf, table, local.at[5]),
    ]
    for copy in copies:
        copy.start()

    barrier = pltpu.get_barrier_semaphore()
    peers = [at(up(0, 1), y, k), at(up(1, 1), y, k), at(z, y, 1 - k)]
    peers += [at(z, near[n], k) for n in (1, 2, 3)]
    peers += [(c, yh * 4 + (x + dx) % 4) for dx in (1, 2, 3)]
    peers += [((z * NY + near[n]) * 2 + k, twin) for n in (0, 1)]
    for peer in peers:
        pl.semaphore_signal(barrier, inc=1, device_id=peer, device_id_type=MESH)
    for copy in copies:
        copy.wait()
    pl.semaphore_wait(barrier, len(peers))

    open_z(WKV)
    open_y(WKV)
    open_z(WB)
    open_z(WO)
    open_z(WQ)
    open_y(WQ)
    tcopy(*tokens_out[1]).start()
    tcopy(*tokens_out[2]).start()

    position = (c * TOK + lax.broadcasted_iota(jnp.int32, (TOK, HEAD), 0)).astype(jnp.float32)
    angle = position * table[...]
    cosine = jnp.cos(angle)
    lane = lax.broadcasted_iota(jnp.int32, (TOK, HEAD), 1)
    sine = jnp.sin(angle) * jnp.where(lane < HEAD // 2, -1.0, 1.0).astype(jnp.float32)

    def turned(piece):
        return (piece * cosine + pltpu.roll(piece, HEAD // 2, 1) * sine).astype(jnp.bfloat16)

    second = (y + 2) % NY

    def second_copy():
        return pltpu.make_async_remote_copy(
            src_ref=wobuf.at[0, z, k], dst_ref=wobuf.at[1, z, k], send_sem=osend.at[0], recv_sem=osend.at[1],
            device_id=at(z, second, k), device_id_type=MESH,
        )

    def take_second():
        second_copy().wait_recv()
        open_z(WP)

    def send_late():
        for n in (1, 2, 3):
            wcopy(n, y).start()

    def take_late():
        for n in (1, 2, 3):
            wcopy(n, near[n]).wait_recv()
        bcopy(WB, 0, k).start()

    def make_keys():
        tok_arrived(twin_l)
        tok_arrived(yh * 4 + (x + 2) % 4)
        tok_arrived(other * 4 + (x + 2) % 4)
        for s in range(NZ):
            paired(WKV, up(0, s))
        both = jnp.zeros((TOK, 2 * HEAD), jnp.float32)
        for s in range(NZ):
            both += jnp.dot(xbuf[s], wkvbuf[s].reshape(512, 2 * HEAD), preferred_element_type=jnp.float32)
        kvbuf[z, y, k, 0] = turned(both[:, :HEAD])
        kvbuf[z, y, k, 1] = both[:, HEAD:].astype(jnp.bfloat16)
        open_z(KV)
        open_y(KV)

    def make_queries():
        bcopy(WB, 0, 1 - k).wait_recv()
        for n in range(NZ):
            zz = up(n % 2, (n + 1) // 2)
            paired(WQ, zz)
            term = jnp.dot(xbuf[zz], wqbuf[zz].reshape(512, 512), preferred_element_type=jnp.float32)
            proj[...] = term if n == 0 else proj[...] + term
        for h in range(HEADS):
            qbuf[pl.ds(h * TOK, TOK), :] = turned(proj[:, pl.ds(h * HEAD, HEAD)])

    rows = 512
    keys = NY * 2 * TOK

    def attend(zz, first=False):
        def some():
            paired(KV, zz)

            def body(i, carry):
                at_rows = pl.ds(pl.multiple_of(i * rows, rows), rows)
                key = kvbuf[zz, :, :, 0].reshape(keys, HEAD)
                value = kvbuf[zz, :, :, 1].reshape(keys, HEAD)
                score = lax.dot_general(
                    qbuf[at_rows, :], key, (((1,), (1,)), ((), ())), preferred_element_type=jnp.float32
                )
                if first:
                    key_at = lax.broadcasted_iota(jnp.int32, (rows, keys), 1)
                    query_at = (y * 2 + k) * TOK + lax.broadcasted_iota(jnp.int32, (rows, keys), 0) % TOK
                    score = jnp.where(key_at <= query_at, score, jnp.float32(-1e30))
                top = jnp.max(score, axis=1, keepdims=True)
                if first:
                    new = jnp.broadcast_to(top, (rows, HEAD))
                else:
                    old = mbuf[at_rows, :]
                    new = jnp.maximum(old, top)
                exps = jnp.exp2(score * SCALE2 - jnp.tile(new * SCALE2, (1, keys // HEAD)))
                total = jnp.sum(exps, axis=1, keepdims=True)
                summed = jnp.dot(exps.astype(jnp.bfloat16), value, preferred_element_type=jnp.float32)
                if first:
                    lbuf[at_rows, :] = jnp.broadcast_to(total, (rows, HEAD))
                    acc[at_rows, :] = summed
                else:
                    factor = jnp.exp2((old - new) * SCALE2)
                    lbuf[at_rows, :] = lbuf[at_rows, :] * factor + total
                    acc[at_rows, :] = acc[at_rows, :] * factor + summed
                mbuf[at_rows, :] = new
                return carry

            lax.fori_loop(0, HEADS * TOK // rows, body, 0)

        if first:
            some()
        else:
            pl.when(zz <= z)(some)

    def acopy(h):
        at_rows = pl.ds(h * HALF, HALF)
        return pltpu.make_async_remote_copy(
            src_ref=abuf.at[0, at_rows], dst_ref=abuf.at[1, at_rows], send_sem=asend.at[0], recv_sem=arecv.at[h],
            device_id=at(z, near[1], k), device_id_type=MESH,
        )

    def finish():
        for h in range(HEADS):
            at_rows = pl.ds(h * TOK, TOK)
            abuf[0, :, pl.ds(h * HEAD, HEAD)] = (acc[at_rows, :] / lbuf[at_rows, :]).astype(jnp.bfloat16)
        for h in (0, 1):
            acopy(h).start()

    step0a(WKV, False)
    step(WB, 1, 0, True)
    step(WO, 1, 0, True)
    step0a(WQ, False)
    step0b(WKV, True)
    step(WB, 2, 0, True)
    step(WKV, 1, 0, False)
    step(WKV, 1, 1, True)
    step(WO, 2, 0, True)
    step0b(WQ, True)
    tcopy(*tokens_out[0]).start()
    second_copy().start()
    step(WB, 3, 0, True)
    step(WKV, 2, 0, False)
    step(WKV, 2, 1, True)
    step(WO, 3, 0, True)
    tok_arrived(xl)
    tcopy(*tokens_out[3]).start()
    tok_arrived(xr)
    step(WB, 4, 0, True)
    send_late()
    step(WKV, 3, 0, False)
    step(WKV, 3, 1, True)
    take_second()
    step(WQ, 1, 0, False)
    step(WQ, 1, 1, True)
    tok_arrived(twin)
    tcopy(*tokens_out[4]).start()
    tcopy(*tokens_out[5]).start()
    step(WKV, 4, 0, False)
    step(WKV, 4, 1, True)
    tok_arrived(twin_r)
    tcopy(*tokens_out[6]).start()
    step(WQ, 2, 0, False)
    step(WQ, 2, 1, True)
    make_keys()
    step(WP, 1, 0, True)
    step(WQ, 3, 0, False)
    step(WQ, 3, 1, True)
    take_late()
    step0a(KV, False)
    step0b(KV, True)
    step(WQ, 4, 0, False)
    step(WQ, 4, 1, True)
    step(KV, 1, 0, False)
    step(KV, 1, 1, True)
    step(WP, 2, 0, True)
    make_queries()
    attend(z, True)
    pl.when(z == 0)(finish)
    step(KV, 2, 0, False)
    step(KV, 2, 1, True)
    attend(up(1, 1))
    attend(up(0, 1))
    pl.when(z == 1)(finish)
    step(KV, 3, 0, False)
    step(KV, 3, 1, True)
    step(WP, 3, 0, True)
    attend(up(1, 2))
    attend(up(0, 2))
    pl.when(z == 2)(finish)
    pl.when(z >= 4)(lambda: step(KV, 4, 0, False))
    pl.when(z >= 4)(lambda: step(KV, 4, 1, True))
    step(WO, 4, 0, True)
    attend(up(1, 3))
    attend(up(0, 3))
    attend(up(1, 4))
    pl.when(z >= 3)(finish)

    def rcopy(q, n, h, dx):
        there = (x + dx) % 4
        return pltpu.make_async_remote_copy(
            src_ref=pbuf.at[q, n, h, :, there], dst_ref=rbuf.at[q, n, h, dx - 1], send_sem=rsend.at[0],
            recv_sem=rrecv.at[q, n, h], device_id=(c, yh * 4 + there), device_id_type=MESH,
        )

    def make_terms(q, n, h):
        terms = lax.dot_general(
            abuf[n, pl.ds(h * HALF, HALF), :], wobuf[q].reshape(1024, 512), (((1,), (1,)), ((), ())),
            preferred_element_type=jnp.float32,
        ).astype(jnp.bfloat16)
        for slot in range(8):
            pbuf[q, n, h, slot // 4, slot % 4] = terms[:, slot * HEAD:(slot + 1) * HEAD]
        for dx in (2, 1, 3):
            rcopy(q, n, h, dx).start()

    def hcopy(q, n, h, j):
        half = (other, yh)[j]
        return pltpu.make_async_remote_copy(
            src_ref=sbuf.at[q, n, h, j], dst_ref=ybuf.at[yh * 4 + (y, second)[q], pl.ds(h * HALF, HALF)],
            send_sem=hsend.at[0], recv_sem=hrecv.at[0],
            device_id=((z * NY + near[n]) * 2 + k, half * 4 + x), device_id_type=MESH,
        )

    def sum_over_x(q, n, h):
        remote(rbuf.at[q, n, h], rsend.at[0], rrecv.at[q, n, h], sibling).wait_recv()
        for j, half in ((0, other), (1, yh)):
            total = pbuf[q, n, h, half, x].astype(jnp.float32)
            for dx in (1, 2, 3):
                total = total + rbuf[q, n, h, dx - 1, half].astype(jnp.float32)
            if n == 0 and j == 1:
                ybuf[yh * 4 + (y, second)[q], pl.ds(h * HALF, HALF), :] = total.astype(jnp.bfloat16)
            else:
                sbuf[q, n, h, j] = total.astype(jnp.bfloat16)
                hcopy(q, n, h, j).start()

    bcopy(WO, 0, 1 - k).wait_recv()
    make_terms(0, 0, 0)
    make_terms(0, 0, 1)
    step(WP, 4, 0, True)
    acopy(0).wait_recv()
    make_terms(0, 1, 0)
    acopy(1).wait_recv()
    make_terms(0, 1, 1)
    sum_over_x(0, 0, 0)
    bcopy(WP, 0, 1 - k).wait_recv()
    make_terms(1, 0, 0)
    sum_over_x(0, 0, 1)
    make_terms(1, 0, 1)
    make_terms(1, 1, 0)
    make_terms(1, 1, 1)
    sum_over_x(0, 1, 0)
    sum_over_x(0, 1, 1)
    sum_over_x(1, 0, 0)
    sum_over_x(1, 0, 1)
    sum_over_x(1, 1, 0)
    sum_over_x(1, 1, 1)
    @pl.when(z < 4)
    def _():
        step(KV, 4, 0, False)
        step(KV, 4, 1, True)

    for g in (WKV, WQ, KV, WO, WB, WP):
        drain(g)
    remote(xbuf.at[pl.ds(0, 7)], tsend.at[0], orecv.at[0, 0], sibling).wait_send()
    remote(abuf.at[0], asend.at[0], orecv.at[0, 0], sibling).wait_send()
    second_copy().wait_send()
    remote(rbuf, rsend.at[0], orecv.at[0, 0], sibling).wait_send()
    remote(ybuf.at[pl.ds(0, 6)], hsend.at[0], hrecv.at[0], sibling).wait_send()
    remote(ybuf.at[pl.ds(0, 6)], hsend.at[0], hrecv.at[0], sibling).wait_recv()
    for n in range(NY):
        out[:, pl.ds(n * HEAD, HEAD)] = (
            ybuf[n].astype(jnp.float32) + ybuf[4 + n].astype(jnp.float32)
        ).astype(jnp.bfloat16)


def body(tokens, w_query, key_matrix, value_matrix, w_out):
    half = HEAD // 2
    inverse_freq = np.power(
        np.float32(500000.0), -np.arange(half, dtype=np.float32) * np.float32(2.0) / np.float32(HEAD)
    ).astype(np.float32)
    table = jnp.asarray(np.concatenate([inverse_freq, inverse_freq])[None, :])
    hbm = pl.BlockSpec(memory_space=pltpu.HBM)
    vmem = pl.BlockSpec(memory_space=pltpu.VMEM)
    bf16, f32 = jnp.bfloat16, jnp.float32
    dma = pltpu.SemaphoreType.DMA
    operands = [
        pltpu.with_memory_space_constraint(a, pltpu.HBM)
        for a in (tokens, w_query, key_matrix, value_matrix, w_out.T, table)
    ]
    return pl.pallas_call(
        kernel,
        out_shape=jax.ShapeDtypeStruct((TOK, 512), bf16),
        in_specs=[hbm] * 6,
        out_specs=vmem,
        scratch_shapes=[
            pltpu.VMEM((8, TOK, 512), bf16),
            pltpu.VMEM((NZ, NY, 2, 64, 2 * HEAD), bf16),
            pltpu.VMEM((NZ, NY, 2, 64, 512), bf16),
            pltpu.VMEM((NZ, NY, 2, 2, TOK, HEAD), bf16),
            pltpu.VMEM((2, NZ, 2, 64, 512), bf16),
            pltpu.VMEM((1, HEAD), f32),
            pltpu.VMEM((HEADS * TOK, HEAD), bf16),
            pltpu.VMEM((TOK, 512), f32),
            pltpu.VMEM((HEADS * TOK, HEAD), f32),
            pltpu.VMEM((HEADS * TOK, HEAD), f32),
            pltpu.VMEM((HEADS * TOK, HEAD), f32),
            pltpu.VMEM((2, TOK, 512), bf16),
            pltpu.VMEM((2, 2, 2, 2, 4, HALF, HEAD), bf16),
            pltpu.VMEM((2, 2, 2, 3, 2, HALF, HEAD), bf16),
            pltpu.VMEM((2, 2, 2, 2, HALF, HEAD), bf16),
            pltpu.VMEM((2 * NY, TOK, HEAD), bf16),
            dma((6,)),
            dma((6,)),
            dma((3,)),
            dma((6,)),
            dma((NZ,)),
            dma((3, NZ, 2)),
            dma((3, 2)),
            dma((6, NZ)),
            dma((3, NZ)),
            dma((1,)),
            dma((8,)),
            dma((1,)),
            dma((NY,)),
            dma((2,)),
            dma((1,)),
            dma((2,)),
            dma((1,)),
            dma((2, 2, 2)),
            dma((1,)),
            dma((1,)),
        ],
        compiler_params=pltpu.CompilerParams(
            collective_id=0, has_side_effects=True, vmem_limit_bytes=50 * 2**20
        ),
    )(*operands)


def solution(mesh):
    in_specs = (
        P("ctx", "fsdp"),
        P("ctx", "fsdp"),
        P("ctx", "fsdp"),
        P("ctx", "fsdp"),
        P("fsdp", "ctx"),
    )
    out_specs = P("ctx", "fsdp")
    return jax.shard_map(body, mesh=mesh, in_specs=in_specs, out_specs=out_specs, check_vma=False)
```

```python
import functools
import math

import jax
import jax.numpy as jnp
import numpy as np
from jax import lax
from jax.experimental import pallas as pl
from jax.experimental.pallas import tpu as pltpu
from jax.sharding import PartitionSpec as P

MESH = pl.DeviceIdType.MESH
HEAD = 128
HEADS = 4
NZ, NY = 8, 4
TOK = 128
HALF = TOK // 2
SCALE2 = math.log2(math.e) / math.sqrt(HEAD)
REACH = ((4, 3), (3, 4))
WKV, WQ, KV, WO, WB, WP = 0, 1, 2, 3, 4, 5
FIRST = 48


def kernel(
    tok, wq, wk, wv, wo, invf, out,
    xbuf, wkvbuf, wqbuf, kvbuf, wobuf, table, qbuf, proj, mbuf, lbuf, acc, abuf, pbuf, rbuf, sbuf, ybuf,
    local, zsend, ysend, bsend, ksend, zrecv, yrecv, brecv, orecv, tsend, trecv, lsend, lrecv, osend, asend, arecv, rsend, rrecv, hsend, hrecv,
):
    c = lax.axis_index("ctx")
    f = lax.axis_index("fsdp")
    k = c % 2
    y = (c // 2) % NY
    z = c // (2 * NY)
    x = f % 4
    yh = f // 4

    def at(zz, yy, kk):
        return ((zz * NY + yy) * 2 + kk, f)

    def up(d, n):
        return (z + (n if d == 0 else NZ - n)) % NZ

    near = (y, y + 1 - 2 * (y % 2), 2 - y // 2, 3 - 3 * (y // 2))
    bufs = (wkvbuf, wqbuf, kvbuf)

    base = (2 * (y // 2), 2 - 2 * (y // 2))

    def remote(ref, send, recv, peer):
        return pltpu.make_async_remote_copy(
            src_ref=ref, dst_ref=ref, send_sem=send, recv_sem=recv, device_id=peer, device_id_type=MESH
        )

    def view(g, zz, yy, kk):
        if g == WQ:
            return wqbuf.at[zz, yy, kk, pl.ds(0, FIRST)]
        return bufs[g].at[zz, yy, kk]

    def late(zz, yy, kk):
        return wqbuf.at[zz, yy, kk, pl.ds(FIRST, 64 - FIRST)]

    def pair(g, zz, p):
        if g == WO:
            return wobuf.at[0, zz, k]
        if g == WP:
            return wobuf.at[1, zz, k]
        if g == WB:
            return late(zz, y, k)
        return view(g, zz, pl.ds(base[p], 2), k)

    def recv_of(g, zz, p):
        return orecv.at[g - WO, zz] if g >= WO else zrecv.at[g, zz, p]

    def zcopy(g, d, step, p):
        zz = up(1 - d, step)
        return remote(pair(g, zz, p), zsend.at[g], recv_of(g, zz, p), at(up(d, 1), y, k))

    def zfirst(g, d, n):
        return remote(view(g, z, near[n], k), zsend.at[g], zrecv.at[g, z, 0], at(up(d, 1), y, k))

    def ycopy(g, n):
        return remote(view(g, z, y, k), ysend.at[g], yrecv.at[g, min(n, 2) - 1], at(z, near[n], k))

    sibling = at(z, y, 1 - k)

    def bcopy(g, zz, kk):
        ref = wobuf.at[g // WP, :, kk] if g in (WO, WP) else late(slice(None), slice(None), kk) if g == WB else view(g, zz, slice(None), kk)
        return remote(ref, ksend.at[zz] if g == KV else bsend.at[g], brecv.at[g, zz], sibling)

    def share(g, zz):
        if g == KV:
            pl.when(zz <= z)(lambda: bcopy(g, zz, k).start())
        else:
            bcopy(g, zz, k).start()

    def paired(g, zz):
        bcopy(g, zz, 1 - k).wait_recv()

    def open_y(g):
        for n in (1, 2, 3):
            ycopy(g, n).start()

    def open_z(g):
        for d in (0, 1):
            if g >= WO:
                zcopy(g, d, 0, 0).start()
            else:
                zfirst(g, d, 0).start()

    def step0a(g, last):
        remote(view(g, z, near[1], k), ysend.at[g], yrecv.at[g, 0], sibling).wait_recv()
        for d in (0, 1):
            zfirst(g, d, 1).start()
        if last:
            bcopy(g, z, k).start()

    def step0b(g, last):
        remote(pair(g, z, 1), ysend.at[g], yrecv.at[g, 1], sibling).wait_recv()
        for d in (0, 1):
            zcopy(g, d, 0, 1).start()
        if last:
            bcopy(g, z, k).start()

    def step(g, s, p, last):
        for d in (0, 1):
            if s <= REACH[d][p]:
                zz = up(1 - d, s)
                remote(pair(g, zz, p), zsend.at[g], recv_of(g, zz, p), sibling).wait_recv()
                if s < REACH[d][p]:
                    zcopy(g, d, s, p).start()
        if g < WO and last:
            share(g, up(1, s))
            if s < 4:
                share(g, up(0, s))
        elif s == 4 and g in (WO, WP):
            bcopy(g, 0, k).start()

    def wcopy(n, yy):
        return remote(late(slice(None), yy, k), lsend.at[0], lrecv.at[yy], at(z, near[n], k))

    def drain(g):
        if g in (WO, WP):
            remote(wobuf.at[0, pl.ds(0, 7), k], zsend.at[g], orecv.at[0, 0], sibling).wait_send()
            bcopy(g, 0, k).wait_send()
            return
        if g == WB:
            remote(late(pl.ds(0, 7), y, k), zsend.at[g], orecv.at[0, 0], sibling).wait_send()
            remote(late(slice(None), pl.ds(0, 3), k), lsend.at[0], orecv.at[0, 0], sibling).wait_send()
            bcopy(g, 0, k).wait_send()
            return
        remote(view(g, pl.ds(0, 7), slice(None), k), zsend.at[g], orecv.at[0, 0], sibling).wait_send()
        remote(view(g, 0, pl.ds(0, 3), k), ysend.at[g], orecv.at[0, 0], sibling).wait_send()
        if g == KV:
            for zz in range(NZ):
                pl.when(zz <= z)(lambda: bcopy(g, zz, k).wait_send())
        else:
            remote(view(g, slice(None), slice(None), k), bsend.at[g], orecv.at[0, 0], sibling).wait_send()

    def tcopy(slot, peer):
        return remote(xbuf.at[slot], tsend.at[0], trecv.at[slot], (c, peer))

    def tok_arrived(slot):
        tcopy(slot, yh * 4 + (x + 1) % 4).wait_recv()

    other = 1 - yh
    xr = yh * 4 + (x + 1) % 4
    xl = yh * 4 + (x + 3) % 4
    twin = other * 4 + x
    twin_l = other * 4 + (x + 3) % 4
    twin_r = other * 4 + (x + 1) % 4
    tokens_out = (
        (f, twin), (f, xr), (f, xl),
        (xl, xr),
        (twin, xr), (twin, xl),
        (twin_r, xl),
    )

    mine = wkvbuf.at[z, y, k]
    copies = [
        pltpu.make_async_copy(wk, mine.at[:, pl.ds(0, HEAD)], local.at[0]),
        pltpu.make_async_copy(wv, mine.at[:, pl.ds(HEAD, HEAD)], local.at[1]),
        pltpu.make_async_copy(wo, wobuf.at[0, z, k], local.at[2]),
        pltpu.make_async_copy(wq, wqbuf.at[z, y, k], local.at[3]),
        pltpu.make_async_copy(tok, xbuf.at[f], local.at[4]),
        pltpu.make_async_copy(invf, table, local.at[5]),
    ]
    for copy in copies:
        copy.start()

    barrier = pltpu.get_barrier_semaphore()
    peers = [at(up(0, 1), y, k), at(up(1, 1), y, k), at(z, y, 1 - k)]
    peers += [at(z, near[n], k) for n in (1, 2, 3)]
    peers += [(c, yh * 4 + (x + dx) % 4) for dx in (1, 2, 3)]
    peers += [((z * NY + near[n]) * 2 + k, twin) for n in (0, 1)]
    for peer in peers:
        pl.semaphore_signal(barrier, inc=1, device_id=peer, device_id_type=MESH)
    for copy in copies:
        copy.wait()
    pl.semaphore_wait(barrier, len(peers))

    open_z(WKV)
    open_y(WKV)
    open_z(WB)
    open_z(WO)
    open_z(WQ)
    open_y(WQ)
    tcopy(*tokens_out[1]).start()
    tcopy(*tokens_out[2]).start()

    position = (c * TOK + lax.broadcasted_iota(jnp.int32, (TOK, HEAD), 0)).astype(jnp.float32)
    angle = position * table[...]
    cosine = jnp.cos(angle)
    lane = lax.broadcasted_iota(jnp.int32, (TOK, HEAD), 1)
    sine = jnp.sin(angle) * jnp.where(lane < HEAD // 2, -1.0, 1.0).astype(jnp.float32)

    def turned(piece):
        return (piece * cosine + pltpu.roll(piece, HEAD // 2, 1) * sine).astype(jnp.bfloat16)

    second = (y + 2) % NY

    def second_copy():
        return pltpu.make_async_remote_copy(
            src_ref=wobuf.at[0, z, k], dst_ref=wobuf.at[1, z, k], send_sem=osend.at[0], recv_sem=osend.at[1],
            device_id=at(z, second, k), device_id_type=MESH,
        )

    def take_second():
        second_copy().wait_recv()
        open_z(WP)

    def send_late():
        for n in (1, 2, 3):
            wcopy(n, y).start()

    def take_late():
        for n in (1, 2, 3):
            wcopy(n, near[n]).wait_recv()
        bcopy(WB, 0, k).start()

    def make_keys():
        tok_arrived(twin_l)
        tok_arrived(yh * 4 + (x + 2) % 4)
        tok_arrived(other * 4 + (x + 2) % 4)
        for s in range(NZ):
            paired(WKV, up(0, s))
        both = jnp.zeros((TOK, 2 * HEAD), jnp.float32)
        for s in range(NZ):
            both += jnp.dot(xbuf[s], wkvbuf[s].reshape(512, 2 * HEAD), preferred_element_type=jnp.float32)
        kvbuf[z, y, k, 0] = turned(both[:, :HEAD])
        kvbuf[z, y, k, 1] = both[:, HEAD:].astype(jnp.bfloat16)
        open_z(KV)
        open_y(KV)

    def make_queries():
        bcopy(WB, 0, 1 - k).wait_recv()
        for n in range(NZ):
            zz = up(n % 2, (n + 1) // 2)
            paired(WQ, zz)
            term = jnp.dot(xbuf[zz], wqbuf[zz].reshape(512, 512), preferred_element_type=jnp.float32)
            proj[...] = term if n == 0 else proj[...] + term
        for h in range(HEADS):
            qbuf[pl.ds(h * TOK, TOK), :] = turned(proj[:, pl.ds(h * HEAD, HEAD)])

    rows = 512
    keys = NY * 2 * TOK

    def attend(zz, first=False):
        def some():
            paired(KV, zz)

            def body(i, carry):
                at_rows = pl.ds(pl.multiple_of(i * rows, rows), rows)
                key = kvbuf[zz, :, :, 0].reshape(keys, HEAD)
                value = kvbuf[zz, :, :, 1].reshape(keys, HEAD)
                score = lax.dot_general(
                    qbuf[at_rows, :], key, (((1,), (1,)), ((), ())), preferred_element_type=jnp.float32
                )
                if first:
                    key_at = lax.broadcasted_iota(jnp.int32, (rows, keys), 1)
                    query_at = (y * 2 + k) * TOK + lax.broadcasted_iota(jnp.int32, (rows, keys), 0) % TOK
                    score = jnp.where(key_at <= query_at, score, jnp.float32(-1e30))
                top = jnp.max(score, axis=1, keepdims=True)
                if first:
                    new = jnp.broadcast_to(top, (rows, HEAD))
                else:
                    old = mbuf[at_rows, :]
                    new = jnp.maximum(old, top)
                exps = jnp.exp2(score * SCALE2 - jnp.tile(new * SCALE2, (1, keys // HEAD)))
                total = jnp.sum(exps, axis=1, keepdims=True)
                summed = jnp.dot(exps.astype(jnp.bfloat16), value, preferred_element_type=jnp.float32)
                if first:
                    lbuf[at_rows, :] = jnp.broadcast_to(total, (rows, HEAD))
                    acc[at_rows, :] = summed
                else:
                    factor = jnp.exp2((old - new) * SCALE2)
                    lbuf[at_rows, :] = lbuf[at_rows, :] * factor + total
                    acc[at_rows, :] = acc[at_rows, :] * factor + summed
                mbuf[at_rows, :] = new
                return carry

            lax.fori_loop(0, HEADS * TOK // rows, body, 0)

        if first:
            some()
        else:
            pl.when(zz <= z)(some)

    def acopy(h):
        at_rows = pl.ds(h * HALF, HALF)
        return pltpu.make_async_remote_copy(
            src_ref=abuf.at[0, at_rows], dst_ref=abuf.at[1, at_rows], send_sem=asend.at[0], recv_sem=arecv.at[h],
            device_id=at(z, near[1], k), device_id_type=MESH,
        )

    def finish():
        for h in range(HEADS):
            at_rows = pl.ds(h * TOK, TOK)
            abuf[0, :, pl.ds(h * HEAD, HEAD)] = (acc[at_rows, :] / lbuf[at_rows, :]).astype(jnp.bfloat16)
        for h in (0, 1):
            acopy(h).start()

    step0a(WKV, False)
    step(WB, 1, 0, True)
    step(WO, 1, 0, True)
    step0a(WQ, False)
    step0b(WKV, True)
    step(WB, 2, 0, True)
    step(WKV, 1, 0, False)
    step(WKV, 1, 1, True)
    step(WO, 2, 0, True)
    step0b(WQ, True)
    tcopy(*tokens_out[0]).start()
    second_copy().start()
    step(WB, 3, 0, True)
    step(WKV, 2, 0, False)
    step(WKV, 2, 1, True)
    step(WO, 3, 0, True)
    tok_arrived(xl)
    tcopy(*tokens_out[3]).start()
    tok_arrived(xr)
    step(WB, 4, 0, True)
    send_late()
    step(WKV, 3, 0, False)
    step(WKV, 3, 1, True)
    take_second()
    step(WQ, 1, 0, False)
    step(WQ, 1, 1, True)
    tok_arrived(twin)
    tcopy(*tokens_out[4]).start()
    tcopy(*tokens_out[5]).start()
    step(WKV, 4, 0, False)
    step(WKV, 4, 1, True)
    tok_arrived(twin_r)
    tcopy(*tokens_out[6]).start()
    step(WQ, 2, 0, False)
    step(WQ, 2, 1, True)
    make_keys()
    step(WP, 1, 0, True)
    step(WO, 4, 0, True)
    step(WQ, 3, 0, False)
    step(WQ, 3, 1, True)
    take_late()
    step0a(KV, False)
    step0b(KV, True)
    step(WQ, 4, 0, False)
    step(WQ, 4, 1, True)
    step(KV, 1, 0, False)
    step(KV, 1, 1, True)
    step(WP, 2, 0, True)
    make_queries()
    attend(z, True)
    pl.when(z == 0)(finish)
    step(KV, 2, 0, False)
    step(KV, 2, 1, True)
    attend(up(1, 1))
    attend(up(0, 1))
    pl.when(z == 1)(finish)
    step(KV, 3, 0, False)
    step(KV, 3, 1, True)
    step(WP, 3, 0, True)
    attend(up(1, 2))
    attend(up(0, 2))
    pl.when(z == 2)(finish)
    attend(up(1, 3))
    attend(up(0, 3))
    pl.when(z >= 4)(lambda: step(KV, 4, 0, False))
    pl.when(z >= 4)(lambda: step(KV, 4, 1, True))
    attend(up(1, 4))
    pl.when(z >= 3)(finish)

    def rcopy(q, n, h, dx):
        there = (x + dx) % 4
        return pltpu.make_async_remote_copy(
            src_ref=pbuf.at[q, n, h, :, there], dst_ref=rbuf.at[q, n, h, dx - 1], send_sem=rsend.at[0],
            recv_sem=rrecv.at[q, n, h], device_id=(c, yh * 4 + there), device_id_type=MESH,
        )

    def make_terms(q, n, h):
        terms = lax.dot_general(
            abuf[n, pl.ds(h * HALF, HALF), :], wobuf[q].reshape(1024, 512), (((1,), (1,)), ((), ())),
            preferred_element_type=jnp.float32,
        ).astype(jnp.bfloat16)
        for slot in range(8):
            pbuf[q, n, h, slot // 4, slot % 4] = terms[:, slot * HEAD:(slot + 1) * HEAD]
        for dx in (2, 1, 3):
            rcopy(q, n, h, dx).start()

    def hcopy(q, n, h, j):
        half = (other, yh)[j]
        return pltpu.make_async_remote_copy(
            src_ref=sbuf.at[q, n, h, j], dst_ref=ybuf.at[yh * 4 + (y, second)[q], pl.ds(h * HALF, HALF)],
            send_sem=hsend.at[0], recv_sem=hrecv.at[0],
            device_id=((z * NY + near[n]) * 2 + k, half * 4 + x), device_id_type=MESH,
        )

    def sum_over_x(q, n, h):
        remote(rbuf.at[q, n, h], rsend.at[0], rrecv.at[q, n, h], sibling).wait_recv()
        for j, half in ((0, other), (1, yh)):
            total = pbuf[q, n, h, half, x].astype(jnp.float32)
            for dx in (1, 2, 3):
                total = total + rbuf[q, n, h, dx - 1, half].astype(jnp.float32)
            if n == 0 and j == 1:
                ybuf[yh * 4 + (y, second)[q], pl.ds(h * HALF, HALF), :] = total.astype(jnp.bfloat16)
            else:
                sbuf[q, n, h, j] = total.astype(jnp.bfloat16)
                hcopy(q, n, h, j).start()

    bcopy(WO, 0, 1 - k).wait_recv()
    make_terms(0, 0, 0)
    make_terms(0, 0, 1)
    step(WP, 4, 0, True)
    acopy(0).wait_recv()
    make_terms(0, 1, 0)
    acopy(1).wait_recv()
    make_terms(0, 1, 1)
    sum_over_x(0, 0, 0)
    bcopy(WP, 0, 1 - k).wait_recv()
    make_terms(1, 0, 0)
    sum_over_x(0, 0, 1)
    make_terms(1, 0, 1)
    make_terms(1, 1, 0)
    make_terms(1, 1, 1)
    sum_over_x(0, 1, 0)
    sum_over_x(0, 1, 1)
    sum_over_x(1, 0, 0)
    sum_over_x(1, 0, 1)
    sum_over_x(1, 1, 0)
    sum_over_x(1, 1, 1)
    @pl.when(z < 4)
    def _():
        step(KV, 4, 0, False)
        step(KV, 4, 1, True)

    for g in (WKV, WQ, KV, WO, WB, WP):
        drain(g)
    remote(xbuf.at[pl.ds(0, 7)], tsend.at[0], orecv.at[0, 0], sibling).wait_send()
    remote(abuf.at[0], asend.at[0], orecv.at[0, 0], sibling).wait_send()
    second_copy().wait_send()
    remote(rbuf, rsend.at[0], orecv.at[0, 0], sibling).wait_send()
    remote(ybuf.at[pl.ds(0, 6)], hsend.at[0], hrecv.at[0], sibling).wait_send()
    remote(ybuf.at[pl.ds(0, 6)], hsend.at[0], hrecv.at[0], sibling).wait_recv()
    for n in range(NY):
        out[:, pl.ds(n * HEAD, HEAD)] = (
            ybuf[n].astype(jnp.float32) + ybuf[4 + n].astype(jnp.float32)
        ).astype(jnp.bfloat16)


def body(tokens, w_query, key_matrix, value_matrix, w_out):
    half = HEAD // 2
    inverse_freq = np.power(
        np.float32(500000.0), -np.arange(half, dtype=np.float32) * np.float32(2.0) / np.float32(HEAD)
    ).astype(np.float32)
    table = jnp.asarray(np.concatenate([inverse_freq, inverse_freq])[None, :])
    hbm = pl.BlockSpec(memory_space=pltpu.HBM)
    vmem = pl.BlockSpec(memory_space=pltpu.VMEM)
    bf16, f32 = jnp.bfloat16, jnp.float32
    dma = pltpu.SemaphoreType.DMA
    operands = [
        pltpu.with_memory_space_constraint(a, pltpu.HBM)
        for a in (tokens, w_query, key_matrix, value_matrix, w_out.T, table)
    ]
    return pl.pallas_call(
        kernel,
        out_shape=jax.ShapeDtypeStruct((TOK, 512), bf16),
        in_specs=[hbm] * 6,
        out_specs=vmem,
        scratch_shapes=[
            pltpu.VMEM((8, TOK, 512), bf16),
            pltpu.VMEM((NZ, NY, 2, 64, 2 * HEAD), bf16),
            pltpu.VMEM((NZ, NY, 2, 64, 512), bf16),
            pltpu.VMEM((NZ, NY, 2, 2, TOK, HEAD), bf16),
            pltpu.VMEM((2, NZ, 2, 64, 512), bf16),
            pltpu.VMEM((1, HEAD), f32),
            pltpu.VMEM((HEADS * TOK, HEAD), bf16),
            pltpu.VMEM((TOK, 512), f32),
            pltpu.VMEM((HEADS * TOK, HEAD), f32),
            pltpu.VMEM((HEADS * TOK, HEAD), f32),
            pltpu.VMEM((HEADS * TOK, HEAD), f32),
            pltpu.VMEM((2, TOK, 512), bf16),
            pltpu.VMEM((2, 2, 2, 2, 4, HALF, HEAD), bf16),
            pltpu.VMEM((2, 2, 2, 3, 2, HALF, HEAD), bf16),
            pltpu.VMEM((2, 2, 2, 2, HALF, HEAD), bf16),
            pltpu.VMEM((2 * NY, TOK, HEAD), bf16),
            dma((6,)),
            dma((6,)),
            dma((3,)),
            dma((6,)),
            dma((NZ,)),
            dma((3, NZ, 2)),
            dma((3, 2)),
            dma((6, NZ)),
            dma((3, NZ)),
            dma((1,)),
            dma((8,)),
            dma((1,)),
            dma((NY,)),
            dma((2,)),
            dma((1,)),
            dma((2,)),
            dma((1,)),
            dma((2, 2, 2)),
            dma((1,)),
            dma((1,)),
        ],
        compiler_params=pltpu.CompilerParams(
            collective_id=0, has_side_effects=True, vmem_limit_bytes=50 * 2**20
        ),
    )(*operands)


def solution(mesh):
    in_specs = (
        P("ctx", "fsdp"),
        P("ctx", "fsdp"),
        P("ctx", "fsdp"),
        P("ctx", "fsdp"),
        P("fsdp", "ctx"),
    )
    out_specs = P("ctx", "fsdp")
    return jax.shard_map(body, mesh=mesh, in_specs=in_specs, out_specs=out_specs, check_vma=False)
```

```python
import functools
import math

import jax
import jax.numpy as jnp
import numpy as np
from jax import lax
from jax.experimental import pallas as pl
from jax.experimental.pallas import tpu as pltpu
from jax.sharding import PartitionSpec as P

MESH = pl.DeviceIdType.MESH
HEAD = 128
HEADS = 4
NZ, NY = 8, 4
TOK = 128
HALF = TOK // 2
SCALE2 = math.log2(math.e) / math.sqrt(HEAD)
REACH = ((4, 3), (3, 4))
WKV, WQ, KV, WO, WB, WP = 0, 1, 2, 3, 4, 5
FIRST = 48


def kernel(
    tok, wq, wk, wv, wo, invf, out,
    xbuf, wkvbuf, wqbuf, kvbuf, wobuf, table, qbuf, proj, mbuf, lbuf, acc, abuf, pbuf, rbuf, sbuf, ybuf,
    local, zsend, ysend, bsend, ksend, zrecv, yrecv, brecv, orecv, tsend, trecv, lsend, lrecv, osend, asend, arecv, rsend, rrecv, hsend, hrecv,
):
    c = lax.axis_index("ctx")
    f = lax.axis_index("fsdp")
    k = c % 2
    y = (c // 2) % NY
    z = c // (2 * NY)
    x = f % 4
    yh = f // 4

    def at(zz, yy, kk):
        return ((zz * NY + yy) * 2 + kk, f)

    def up(d, n):
        return (z + (n if d == 0 else NZ - n)) % NZ

    near = (y, y + 1 - 2 * (y % 2), 2 - y // 2, 3 - 3 * (y // 2))
    bufs = (wkvbuf, wqbuf, kvbuf)

    base = (2 * (y // 2), 2 - 2 * (y // 2))

    def remote(ref, send, recv, peer):
        return pltpu.make_async_remote_copy(
            src_ref=ref, dst_ref=ref, send_sem=send, recv_sem=recv, device_id=peer, device_id_type=MESH
        )

    def view(g, zz, yy, kk):
        if g == WQ:
            return wqbuf.at[zz, yy, kk, pl.ds(0, FIRST)]
        return bufs[g].at[zz, yy, kk]

    def late(zz, yy, kk):
        return wqbuf.at[zz, yy, kk, pl.ds(FIRST, 64 - FIRST)]

    def pair(g, zz, p):
        if g == WO:
            return wobuf.at[0, zz, k]
        if g == WP:
            return wobuf.at[1, zz, k]
        if g == WB:
            return late(zz, y, k)
        return view(g, zz, pl.ds(base[p], 2), k)

    def recv_of(g, zz, p):
        return orecv.at[g - WO, zz] if g >= WO else zrecv.at[g, zz, p]

    def zcopy(g, d, step, p):
        zz = up(1 - d, step)
        return remote(pair(g, zz, p), zsend.at[g], recv_of(g, zz, p), at(up(d, 1), y, k))

    def zfirst(g, d, n):
        return remote(view(g, z, near[n], k), zsend.at[g], zrecv.at[g, z, 0], at(up(d, 1), y, k))

    def ycopy(g, n):
        return remote(view(g, z, y, k), ysend.at[g], yrecv.at[g, min(n, 2) - 1], at(z, near[n], k))

    sibling = at(z, y, 1 - k)

    def bcopy(g, zz, kk):
        ref = wobuf.at[g // WP, :, kk] if g in (WO, WP) else late(slice(None), slice(None), kk) if g == WB else view(g, zz, slice(None), kk)
        return remote(ref, ksend.at[zz] if g == KV else bsend.at[g], brecv.at[g, zz], sibling)

    def share(g, zz):
        if g == KV:
            pl.when(zz <= z)(lambda: bcopy(g, zz, k).start())
        else:
            bcopy(g, zz, k).start()

    def paired(g, zz):
        bcopy(g, zz, 1 - k).wait_recv()

    def open_y(g):
        for n in (1, 2, 3):
            ycopy(g, n).start()

    def open_z(g):
        for d in (0, 1):
            if g >= WO:
                zcopy(g, d, 0, 0).start()
            else:
                zfirst(g, d, 0).start()

    def step0a(g, last):
        remote(view(g, z, near[1], k), ysend.at[g], yrecv.at[g, 0], sibling).wait_recv()
        for d in (0, 1):
            zfirst(g, d, 1).start()
        if last:
            bcopy(g, z, k).start()

    def step0b(g, last):
        remote(pair(g, z, 1), ysend.at[g], yrecv.at[g, 1], sibling).wait_recv()
        for d in (0, 1):
            zcopy(g, d, 0, 1).start()
        if last:
            bcopy(g, z, k).start()

    def step(g, s, p, last):
        for d in (0, 1):
            if s <= REACH[d][p]:
                zz = up(1 - d, s)
                remote(pair(g, zz, p), zsend.at[g], recv_of(g, zz, p), sibling).wait_recv()
                if s < REACH[d][p]:
                    zcopy(g, d, s, p).start()
        if g < WO and last:
            share(g, up(1, s))
            if s < 4:
                share(g, up(0, s))
        elif s == 4 and g in (WO, WP):
            bcopy(g, 0, k).start()

    def wcopy(n, yy):
        return remote(late(slice(None), yy, k), lsend.at[0], lrecv.at[yy], at(z, near[n], k))

    def drain(g):
        if g in (WO, WP):
            remote(wobuf.at[0, pl.ds(0, 7), k], zsend.at[g], orecv.at[0, 0], sibling).wait_send()
            bcopy(g, 0, k).wait_send()
            return
        if g == WB:
            remote(late(pl.ds(0, 7), y, k), zsend.at[g], orecv.at[0, 0], sibling).wait_send()
            remote(late(slice(None), pl.ds(0, 3), k), lsend.at[0], orecv.at[0, 0], sibling).wait_send()
            bcopy(g, 0, k).wait_send()
            return
        remote(view(g, pl.ds(0, 7), slice(None), k), zsend.at[g], orecv.at[0, 0], sibling).wait_send()
        remote(view(g, 0, pl.ds(0, 3), k), ysend.at[g], orecv.at[0, 0], sibling).wait_send()
        if g == KV:
            for zz in range(NZ):
                pl.when(zz <= z)(lambda: bcopy(g, zz, k).wait_send())
        else:
            remote(view(g, slice(None), slice(None), k), bsend.at[g], orecv.at[0, 0], sibling).wait_send()

    def tcopy(slot, peer):
        return remote(xbuf.at[slot], tsend.at[0], trecv.at[slot], (c, peer))

    def tok_arrived(slot):
        tcopy(slot, yh * 4 + (x + 1) % 4).wait_recv()

    other = 1 - yh
    xr = yh * 4 + (x + 1) % 4
    xl = yh * 4 + (x + 3) % 4
    twin = other * 4 + x
    twin_l = other * 4 + (x + 3) % 4
    twin_r = other * 4 + (x + 1) % 4
    tokens_out = (
        (f, twin), (f, xr), (f, xl),
        (xl, xr),
        (twin, xr), (twin, xl),
        (twin_r, xl),
    )

    mine = wkvbuf.at[z, y, k]
    copies = [
        pltpu.make_async_copy(wk, mine.at[:, pl.ds(0, HEAD)], local.at[0]),
        pltpu.make_async_copy(wv, mine.at[:, pl.ds(HEAD, HEAD)], local.at[1]),
        pltpu.make_async_copy(wo, wobuf.at[0, z, k], local.at[2]),
        pltpu.make_async_copy(wq, wqbuf.at[z, y, k], local.at[3]),
        pltpu.make_async_copy(tok, xbuf.at[f], local.at[4]),
        pltpu.make_async_copy(invf, table, local.at[5]),
    ]
    for copy in copies:
        copy.start()

    barrier = pltpu.get_barrier_semaphore()
    peers = [at(up(0, 1), y, k), at(up(1, 1), y, k), at(z, y, 1 - k)]
    peers += [at(z, near[n], k) for n in (1, 2, 3)]
    peers += [(c, yh * 4 + (x + dx) % 4) for dx in (1, 2, 3)]
    peers += [((z * NY + near[n]) * 2 + k, twin) for n in (0, 1)]
    for peer in peers:
        pl.semaphore_signal(barrier, inc=1, device_id=peer, device_id_type=MESH)
    for copy in copies:
        copy.wait()
    pl.semaphore_wait(barrier, len(peers))

    open_z(WKV)
    open_y(WKV)
    open_z(WB)
    open_z(WO)
    open_z(WQ)
    open_y(WQ)
    tcopy(*tokens_out[1]).start()
    tcopy(*tokens_out[2]).start()

    position = (c * TOK + lax.broadcasted_iota(jnp.int32, (TOK, HEAD), 0)).astype(jnp.float32)
    angle = position * table[...]
    cosine = jnp.cos(angle)
    lane = lax.broadcasted_iota(jnp.int32, (TOK, HEAD), 1)
    sine = jnp.sin(angle) * jnp.where(lane < HEAD // 2, -1.0, 1.0).astype(jnp.float32)

    def turned(piece):
        return (piece * cosine + pltpu.roll(piece, HEAD // 2, 1) * sine).astype(jnp.bfloat16)

    second = (y + 2) % NY

    def second_copy():
        return pltpu.make_async_remote_copy(
            src_ref=wobuf.at[0, z, k], dst_ref=wobuf.at[1, z, k], send_sem=osend.at[0], recv_sem=osend.at[1],
            device_id=at(z, second, k), device_id_type=MESH,
        )

    def take_second():
        second_copy().wait_recv()
        open_z(WP)

    def send_late():
        for n in (1, 2, 3):
            wcopy(n, y).start()

    def take_late():
        for n in (1, 2, 3):
            wcopy(n, near[n]).wait_recv()
        bcopy(WB, 0, k).start()

    def make_keys():
        tok_arrived(twin_l)
        tok_arrived(yh * 4 + (x + 2) % 4)
        tok_arrived(other * 4 + (x + 2) % 4)
        for s in range(NZ):
            paired(WKV, up(0, s))
        both = jnp.zeros((TOK, 2 * HEAD), jnp.float32)
        for s in range(NZ):
            both += jnp.dot(xbuf[s], wkvbuf[s].reshape(512, 2 * HEAD), preferred_element_type=jnp.float32)
        kvbuf[z, y, k, 0] = turned(both[:, :HEAD])
        kvbuf[z, y, k, 1] = both[:, HEAD:].astype(jnp.bfloat16)
        open_z(KV)
        open_y(KV)

    def make_queries():
        bcopy(WB, 0, 1 - k).wait_recv()
        for n in range(NZ):
            zz = up(n % 2, (n + 1) // 2)
            paired(WQ, zz)
            term = jnp.dot(xbuf[zz], wqbuf[zz].reshape(512, 512), preferred_element_type=jnp.float32)
            proj[...] = term if n == 0 else proj[...] + term
        for h in range(HEADS):
            qbuf[pl.ds(h * TOK, TOK), :] = turned(proj[:, pl.ds(h * HEAD, HEAD)])

    rows = 512
    keys = NY * 2 * TOK

    def attend(zz, first=False):
        def some():
            paired(KV, zz)

            def body(i, carry):
                at_rows = pl.ds(pl.multiple_of(i * rows, rows), rows)
                key = kvbuf[zz, :, :, 0].reshape(keys, HEAD)
                value = kvbuf[zz, :, :, 1].reshape(keys, HEAD)
                score = lax.dot_general(
                    qbuf[at_rows, :], key, (((1,), (1,)), ((), ())), preferred_element_type=jnp.float32
                )
                if first:
                    key_at = lax.broadcasted_iota(jnp.int32, (rows, keys), 1)
                    query_at = (y * 2 + k) * TOK + lax.broadcasted_iota(jnp.int32, (rows, keys), 0) % TOK
                    score = jnp.where(key_at <= query_at, score, jnp.float32(-1e30))
                top = jnp.max(score, axis=1, keepdims=True)
                if first:
                    new = jnp.broadcast_to(top, (rows, HEAD))
                else:
                    old = mbuf[at_rows, :]
                    new = jnp.maximum(old, top)
                exps = jnp.exp2(score * SCALE2 - jnp.tile(new * SCALE2, (1, keys // HEAD)))
                total = jnp.sum(exps, axis=1, keepdims=True)
                summed = jnp.dot(exps.astype(jnp.bfloat16), value, preferred_element_type=jnp.float32)
                if first:
                    lbuf[at_rows, :] = jnp.broadcast_to(total, (rows, HEAD))
                    acc[at_rows, :] = summed
                else:
                    factor = jnp.exp2((old - new) * SCALE2)
                    lbuf[at_rows, :] = lbuf[at_rows, :] * factor + total
                    acc[at_rows, :] = acc[at_rows, :] * factor + summed
                mbuf[at_rows, :] = new
                return carry

            lax.fori_loop(0, HEADS * TOK // rows, body, 0)

        if first:
            some()
        else:
            pl.when(zz <= z)(some)

    def acopy(h):
        at_rows = pl.ds(h * HALF, HALF)
        return pltpu.make_async_remote_copy(
            src_ref=abuf.at[0, at_rows], dst_ref=abuf.at[1, at_rows], send_sem=asend.at[0], recv_sem=arecv.at[h],
            device_id=at(z, near[1], k), device_id_type=MESH,
        )

    def finish():
        for h in range(HEADS):
            at_rows = pl.ds(h * TOK, TOK)
            abuf[0, :, pl.ds(h * HEAD, HEAD)] = (acc[at_rows, :] / lbuf[at_rows, :]).astype(jnp.bfloat16)
        for h in (0, 1):
            acopy(h).start()

    step0a(WKV, False)
    step(WB, 1, 0, True)
    step(WO, 1, 0, True)
    step0a(WQ, False)
    step0b(WKV, True)
    step(WB, 2, 0, True)
    step(WKV, 1, 0, False)
    step(WKV, 1, 1, True)
    step(WO, 2, 0, True)
    step0b(WQ, True)
    tcopy(*tokens_out[0]).start()
    second_copy().start()
    step(WB, 3, 0, True)
    step(WKV, 2, 0, False)
    step(WKV, 2, 1, True)
    step(WO, 3, 0, True)
    tok_arrived(xl)
    tcopy(*tokens_out[3]).start()
    tok_arrived(xr)
    step(WB, 4, 0, True)
    send_late()
    step(WKV, 3, 0, False)
    step(WKV, 3, 1, True)
    take_second()
    step(WQ, 1, 0, False)
    step(WQ, 1, 1, True)
    tok_arrived(twin)
    tcopy(*tokens_out[4]).start()
    tcopy(*tokens_out[5]).start()
    step(WKV, 4, 0, False)
    step(WKV, 4, 1, True)
    tok_arrived(twin_r)
    tcopy(*tokens_out[6]).start()
    step(WQ, 2, 0, False)
    step(WQ, 2, 1, True)
    make_keys()
    step(WP, 1, 0, True)
    step(WO, 4, 0, True)
    step(WQ, 3, 0, False)
    step(WQ, 3, 1, True)
    take_late()
    step0a(KV, False)
    step0b(KV, True)
    step(WQ, 4, 0, False)
    step(WQ, 4, 1, True)
    step(KV, 1, 0, False)
    step(KV, 1, 1, True)
    make_queries()
    attend(z, True)
    pl.when(z == 0)(finish)
    step(KV, 2, 0, False)
    step(KV, 2, 1, True)
    step(WP, 2, 0, True)
    attend(up(1, 1))
    attend(up(0, 1))
    pl.when(z == 1)(finish)
    step(KV, 3, 0, False)
    step(KV, 3, 1, True)
    step(WP, 3, 0, True)
    attend(up(1, 2))
    attend(up(0, 2))
    pl.when(z == 2)(finish)
    attend(up(1, 3))
    attend(up(0, 3))
    pl.when(z >= 4)(lambda: step(KV, 4, 0, False))
    pl.when(z >= 4)(lambda: step(KV, 4, 1, True))
    attend(up(1, 4))
    pl.when(z >= 3)(finish)

    def rcopy(q, n, h, dx):
        there = (x + dx) % 4
        return pltpu.make_async_remote_copy(
            src_ref=pbuf.at[q, n, h, :, there], dst_ref=rbuf.at[q, n, h, dx - 1], send_sem=rsend.at[0],
            recv_sem=rrecv.at[q, n, h], device_id=(c, yh * 4 + there), device_id_type=MESH,
        )

    def make_terms(q, n, h):
        terms = lax.dot_general(
            abuf[n, pl.ds(h * HALF, HALF), :], wobuf[q].reshape(1024, 512), (((1,), (1,)), ((), ())),
            preferred_element_type=jnp.float32,
        ).astype(jnp.bfloat16)
        for slot in range(8):
            pbuf[q, n, h, slot // 4, slot % 4] = terms[:, slot * HEAD:(slot + 1) * HEAD]
        for dx in (2, 1, 3):
            rcopy(q, n, h, dx).start()

    def hcopy(q, n, h, j):
        half = (other, yh)[j]
        return pltpu.make_async_remote_copy(
            src_ref=sbuf.at[q, n, h, j], dst_ref=ybuf.at[yh * 4 + (y, second)[q], pl.ds(h * HALF, HALF)],
            send_sem=hsend.at[0], recv_sem=hrecv.at[0],
            device_id=((z * NY + near[n]) * 2 + k, half * 4 + x), device_id_type=MESH,
        )

    def sum_over_x(q, n, h):
        remote(rbuf.at[q, n, h], rsend.at[0], rrecv.at[q, n, h], sibling).wait_recv()
        for j, half in ((0, other), (1, yh)):
            total = pbuf[q, n, h, half, x].astype(jnp.float32)
            for dx in (1, 2, 3):
                total = total + rbuf[q, n, h, dx - 1, half].astype(jnp.float32)
            if n == 0 and j == 1:
                ybuf[yh * 4 + (y, second)[q], pl.ds(h * HALF, HALF), :] = total.astype(jnp.bfloat16)
            else:
                sbuf[q, n, h, j] = total.astype(jnp.bfloat16)
                hcopy(q, n, h, j).start()

    bcopy(WO, 0, 1 - k).wait_recv()
    make_terms(0, 0, 0)
    make_terms(0, 0, 1)
    step(WP, 4, 0, True)
    acopy(0).wait_recv()
    make_terms(0, 1, 0)
    acopy(1).wait_recv()
    make_terms(0, 1, 1)
    sum_over_x(0, 0, 0)
    bcopy(WP, 0, 1 - k).wait_recv()
    make_terms(1, 0, 0)
    sum_over_x(0, 0, 1)
    make_terms(1, 0, 1)
    make_terms(1, 1, 0)
    make_terms(1, 1, 1)
    sum_over_x(0, 1, 0)
    sum_over_x(0, 1, 1)
    sum_over_x(1, 0, 0)
    sum_over_x(1, 0, 1)
    sum_over_x(1, 1, 0)
    sum_over_x(1, 1, 1)
    @pl.when(z < 4)
    def _():
        step(KV, 4, 0, False)
        step(KV, 4, 1, True)

    for g in (WKV, WQ, KV, WO, WB, WP):
        drain(g)
    remote(xbuf.at[pl.ds(0, 7)], tsend.at[0], orecv.at[0, 0], sibling).wait_send()
    remote(abuf.at[0], asend.at[0], orecv.at[0, 0], sibling).wait_send()
    second_copy().wait_send()
    remote(rbuf, rsend.at[0], orecv.at[0, 0], sibling).wait_send()
    remote(ybuf.at[pl.ds(0, 6)], hsend.at[0], hrecv.at[0], sibling).wait_send()
    remote(ybuf.at[pl.ds(0, 6)], hsend.at[0], hrecv.at[0], sibling).wait_recv()
    for n in range(NY):
        out[:, pl.ds(n * HEAD, HEAD)] = (
            ybuf[n].astype(jnp.float32) + ybuf[4 + n].astype(jnp.float32)
        ).astype(jnp.bfloat16)


def body(tokens, w_query, key_matrix, value_matrix, w_out):
    half = HEAD // 2
    inverse_freq = np.power(
        np.float32(500000.0), -np.arange(half, dtype=np.float32) * np.float32(2.0) / np.float32(HEAD)
    ).astype(np.float32)
    table = jnp.asarray(np.concatenate([inverse_freq, inverse_freq])[None, :])
    hbm = pl.BlockSpec(memory_space=pltpu.HBM)
    vmem = pl.BlockSpec(memory_space=pltpu.VMEM)
    bf16, f32 = jnp.bfloat16, jnp.float32
    dma = pltpu.SemaphoreType.DMA
    operands = [
        pltpu.with_memory_space_constraint(a, pltpu.HBM)
        for a in (tokens, w_query, key_matrix, value_matrix, w_out.T, table)
    ]
    return pl.pallas_call(
        kernel,
        out_shape=jax.ShapeDtypeStruct((TOK, 512), bf16),
        in_specs=[hbm] * 6,
        out_specs=vmem,
        scratch_shapes=[
            pltpu.VMEM((8, TOK, 512), bf16),
            pltpu.VMEM((NZ, NY, 2, 64, 2 * HEAD), bf16),
            pltpu.VMEM((NZ, NY, 2, 64, 512), bf16),
            pltpu.VMEM((NZ, NY, 2, 2, TOK, HEAD), bf16),
            pltpu.VMEM((2, NZ, 2, 64, 512), bf16),
            pltpu.VMEM((1, HEAD), f32),
            pltpu.VMEM((HEADS * TOK, HEAD), bf16),
            pltpu.VMEM((TOK, 512), f32),
            pltpu.VMEM((HEADS * TOK, HEAD), f32),
            pltpu.VMEM((HEADS * TOK, HEAD), f32),
            pltpu.VMEM((HEADS * TOK, HEAD), f32),
            pltpu.VMEM((2, TOK, 512), bf16),
            pltpu.VMEM((2, 2, 2, 2, 4, HALF, HEAD), bf16),
            pltpu.VMEM((2, 2, 2, 3, 2, HALF, HEAD), bf16),
            pltpu.VMEM((2, 2, 2, 2, HALF, HEAD), bf16),
            pltpu.VMEM((2 * NY, TOK, HEAD), bf16),
            dma((6,)),
            dma((6,)),
            dma((3,)),
            dma((6,)),
            dma((NZ,)),
            dma((3, NZ, 2)),
            dma((3, 2)),
            dma((6, NZ)),
            dma((3, NZ)),
            dma((1,)),
            dma((8,)),
            dma((1,)),
            dma((NY,)),
            dma((2,)),
            dma((1,)),
            dma((2,)),
            dma((1,)),
            dma((2, 2, 2)),
            dma((1,)),
            dma((1,)),
        ],
        compiler_params=pltpu.CompilerParams(
            collective_id=0, has_side_effects=True, vmem_limit_bytes=50 * 2**20
        ),
    )(*operands)


def solution(mesh):
    in_specs = (
        P("ctx", "fsdp"),
        P("ctx", "fsdp"),
        P("ctx", "fsdp"),
        P("ctx", "fsdp"),
        P("fsdp", "ctx"),
    )
    out_specs = P("ctx", "fsdp")
    return jax.shard_map(body, mesh=mesh, in_specs=in_specs, out_specs=out_specs, check_vma=False)
```
